32 devices in a mesh: dp: 4 (over y, x), ctx: 2 (over core), zero: 4 (over z).
Axes of the slice: x: 2, y: 2, z: 4, core: 2. Of those that a mesh axis runs over, the one named last changes fastest.
Arguments:
- inputs: bfloat16 [16, 256, 640], P(('dp', 'zero'), 'ctx'), may hold values from -6 to 6
- cotangent: bfloat16 [16, 256, 640], P(('dp', 'zero'), 'ctx'), may hold values from -6 to 6
- params: float32 [5573632], P(('ctx', 'zero')), may hold values from -1 to 1
- first_moment: float32 [5573632], P(('ctx', 'zero')), may hold values from -1 to 1
- second_moment: float32 [5573632], P(('ctx', 'zero')), may hold values from 0.0005 to 0.005
Outputs:
- outputs: bfloat16 [16, 256, 640], P(('dp', 'zero'), 'ctx')
- input_grad: float32 [16, 256, 640], P(('dp', 'zero'), 'ctx')
- new_params: float32 [5573632], P(('ctx', 'zero'))
- new_first: float32 [5573632], P(('ctx', 'zero'))
- new_second: float32 [5573632], P(('ctx', 'zero'))
- grads: float32 [5573632], P(('ctx', 'zero'))
The draws below stay inside these ranges and needn't reach their ends.
All inputs are finite; a program needn't handle non-finite values.
Results may differ from the reference program's by a relative error of at most 0.012.
The reference program's roundings to bfloat16 on the way count: a program that leaves them out, or rounds other values in their place, can miss the bound.
Values may be sent and summed in bfloat16 or wider, within the bound.
A program may use at most 192 MiB of HBM per device.

```python
import math
import jax
import jax.numpy as jnp
from jax import lax

D = 640
HQ = 4
HD = 256
FF = 2048
SEQS = 16
LENGTH = 256
PARAMS = 5573632


def draw_params(key, part):
    scales = [D ** (-0.5), D ** (-0.5), D ** (-0.5), (HQ * HD) ** (-0.5), D ** (-0.5), D ** (-0.5), FF ** (-0.5), 0.06, 0.06]
    amounts = [D * HQ * HD, D * HD, D * HD, HQ * HD * D, D * FF, D * FF, FF * D, 4 * D, 2 * HD]
    pieces = []
    for number in range(9):
        subkey = jax.random.fold_in(key, 11 + number)
        drawn = jnp.clip(jax.random.normal(subkey, (amounts[number],), jnp.float32), -3.0, 3.0)
        pieces.append(drawn * scales[number])
    return jnp.concatenate(pieces)


def steps_of(stream_key, shape, shards, least, high):
    gain = 1.0
    for dim, blocks in shards:
        steps = jax.random.uniform(jax.random.fold_in(jax.random.fold_in(stream_key, 6), dim), (blocks,), jnp.float32, least / len(shards), high / len(shards))
        gain = gain * jnp.repeat(jnp.exp(steps), shape[dim] // blocks).reshape((-1,) + (1,) * (len(shape) - 1 - dim))
    return gain


def scatter_about(key, shape, spread, limit, split=(), kind=jnp.bfloat16):
    array = jax.random.normal(key, shape, jnp.float32) * spread
    if len(split) > 0:
        array = steps_of(key, shape, split, -0.22, 0.18) * array
    return jnp.clip(array, min=-limit, max=limit).astype(kind)


def setup_inputs(seed: int = 0) -> dict:
    splits = jax.random.split(jax.random.key(seed), 6)
    return {
        "inputs": scatter_about(splits[0], (SEQS, LENGTH, D), 1.0, 6.0, ((0, 16), (1, 2))),
        "cotangent": scatter_about(splits[1], (SEQS, LENGTH, D), 1.0, 6.0, ((0, 16), (1, 2))),
        "params": draw_params(jax.random.fold_in(splits[5], 71), 0),
        "first_moment": scatter_about(splits[3], (PARAMS,), 0.2, 1.0, ((0, 8),), jnp.float32),
        "second_moment": jnp.clip(jnp.exp(math.log(0.005) - 2.30258502 * jax.random.uniform(splits[4], (PARAMS,), jnp.float32) ** steps_of(splits[4], (PARAMS,), ((0, 8),), -0.2, 0.2)), 0.0005, 0.005),
    }


norm_eps = 1e-06
rope_base = 1000000.0
beta_one = 0.9
beta_two = 0.999
learn_rate = 0.01
decay_rate = 0.1
adam_eps = 1e-08
adam_step = 3
gelu_coef = 0.7978845608028654

def gelu_value(pre_act):
    tanh_part = jnp.tanh(gelu_coef * (pre_act + 0.044715 * pre_act * pre_act * pre_act))
    return 0.5 * pre_act * (1.0 + tanh_part)

def gelu_slope(pre_act):
    tanh_part = jnp.tanh(gelu_coef * (pre_act + 0.044715 * pre_act * pre_act * pre_act))
    return 0.5 * (1.0 + tanh_part) + 0.5 * pre_act * (1.0 - tanh_part * tanh_part) * gelu_coef * (1.0 + 3.0 * 0.044715 * pre_act * pre_act)

def rms_forward(values_in, gain_row):
    inv_rms = lax.rsqrt(lax.optimization_barrier(jnp.mean(values_in * values_in, axis=-1, keepdims=True)) + norm_eps)
    return (values_in * inv_rms * (1.0 + gain_row), inv_rms)

def rms_backward(values_in, inv_rms, gain_row, grad_out):
    weighted = grad_out * (1.0 + gain_row)
    grad_in = inv_rms * (weighted - values_in * inv_rms * inv_rms * lax.optimization_barrier(jnp.mean(weighted * values_in, axis=-1, keepdims=True)))
    leading = tuple(range(values_in.ndim - 1))
    grad_gain = lax.optimization_barrier(jnp.sum(grad_out * values_in * inv_rms, axis=leading))
    return (grad_in, grad_gain)

def rotary_tables(positions, head_dim):
    half_dim = head_dim // 2
    freqs = jnp.exp(jnp.arange(half_dim, dtype=jnp.float32) * (-2.0 * math.log(rope_base) / head_dim))
    angles = positions.astype(jnp.float32)[:, None] * freqs[None, :]
    return (jnp.cos(angles), jnp.sin(angles))

def rotate(tensor, cos_part, sin_part):
    half_dim = tensor.shape[-1] // 2
    first_half = tensor[..., :half_dim]
    second_half = tensor[..., half_dim:]
    return jnp.concatenate([first_half * cos_part - second_half * sin_part, second_half * cos_part + first_half * sin_part], axis=-1)

def rotate_back(tensor, cos_part, sin_part):
    half_dim = tensor.shape[-1] // 2
    first_half = tensor[..., :half_dim]
    second_half = tensor[..., half_dim:]
    return jnp.concatenate([first_half * cos_part + second_half * sin_part, second_half * cos_part - first_half * sin_part], axis=-1)

def unpack(flat_values, model_width, head_count, head_dim, hidden):
    layouts = [(model_width, head_count * head_dim), (model_width, head_dim), (model_width, head_dim), (head_count * head_dim, model_width), (model_width, hidden), (model_width, hidden), (hidden, model_width), (4, model_width), (2, head_dim)]
    pieces = []
    offset = 0
    for layout in layouts:
        amount = layout[0] * layout[1]
        pieces.append(flat_values[offset:offset + amount].reshape(layout))
        offset += amount
    return pieces

def adam_update(weights, moment_one, moment_two, grad_values, clip_scale):
    clipped = grad_values * clip_scale
    new_one = beta_one * moment_one + (1.0 - beta_one) * clipped
    new_two = beta_two * moment_two + (1.0 - beta_two) * clipped * clipped
    corrected_one = new_one / (1.0 - beta_one ** adam_step)
    corrected_two = new_two / (1.0 - beta_two ** adam_step)
    new_weights = weights - learn_rate * (corrected_one / (jnp.sqrt(corrected_two) + adam_eps) + decay_rate * weights)
    return (new_weights, new_one, new_two)

def score_block(query_blk, key_rows, query_pos, key_pos):
    scores = jnp.einsum('thd,sd->hts', query_blk.astype(jnp.float32), key_rows.astype(jnp.float32))
    causal = key_pos[None, None, :] <= query_pos[None, :, None]
    return (scores, causal)

def sequence_pass(input_seq, grad_seq, weights):
    w_query, w_key, w_value, w_out, w_gate, w_up, w_down, norm_gains, head_gains = weights
    norm_gains = norm_gains.astype(jnp.float32)
    head_gains = head_gains.astype(jnp.float32)
    length = input_seq.shape[0]
    positions = jnp.arange(length, dtype=jnp.int32)
    cos_tab, sin_tab = rotary_tables(positions, HD)
    input_rows = input_seq.astype(jnp.float32)
    normed_in, in_scale = rms_forward(input_rows, norm_gains[0])
    normed_b = normed_in.astype(jnp.bfloat16)
    queries = jnp.dot(normed_b, w_query, preferred_element_type=jnp.float32).reshape(length, HQ, HD)
    key_pre = jnp.dot(normed_b, w_key, preferred_element_type=jnp.float32)
    values = jnp.dot(normed_b, w_value, preferred_element_type=jnp.float32)
    q_normed, q_scale = rms_forward(queries, head_gains[0])
    k_normed, k_scale = rms_forward(key_pre, head_gains[1])
    query_scale = HD ** (-0.5)
    q_rot = (rotate(q_normed, cos_tab[:, None, :], sin_tab[:, None, :]) * query_scale).astype(jnp.bfloat16)
    k_rot = rotate(k_normed, cos_tab, sin_tab).astype(jnp.bfloat16)
    v_rows = values.astype(jnp.bfloat16)
    block_rows = math.gcd(length, 512)
    blocks = length // block_rows
    q_blocks = q_rot.reshape(blocks, block_rows, HQ, HD)
    pos_blocks = positions.reshape(blocks, block_rows)

    def forward_block(operands):
        query_blk, pos_blk = operands
        scores, causal = score_block(query_blk, k_rot, pos_blk, positions)
        row_total = lax.optimization_barrier(jnp.sum(jnp.where(causal, jnp.exp(scores), 0.0), axis=-1))
        log_total = jnp.log(row_total)
        attn_probs = jnp.where(causal, jnp.exp(scores - log_total[..., None]), 0.0).astype(jnp.bfloat16)
        attended = jnp.einsum('hts,sd->thd', attn_probs.astype(jnp.float32), v_rows.astype(jnp.float32))
        return (attended, log_total)
    attended, log_totals = lax.map(forward_block, (q_blocks, pos_blocks))
    attn_b = attended.reshape(length, HQ * HD).astype(jnp.bfloat16)
    attn_proj = jnp.dot(attn_b, w_out, preferred_element_type=jnp.float32)
    attn_normed, attn_scale = rms_forward(attn_proj, norm_gains[1])
    hidden_one = input_rows + attn_normed
    ffn_in, ffn_scale = rms_forward(hidden_one, norm_gains[2])
    ffn_b = ffn_in.astype(jnp.bfloat16)
    gate_pre = jnp.dot(ffn_b, w_gate, preferred_element_type=jnp.float32)
    up_proj = jnp.dot(ffn_b, w_up, preferred_element_type=jnp.float32)
    activated = gelu_value(gate_pre)
    mixed_b = (activated * up_proj).astype(jnp.bfloat16)
    ffn_proj = jnp.dot(mixed_b, w_down, preferred_element_type=jnp.float32)
    ffn_normed, out_scale = rms_forward(ffn_proj, norm_gains[3])
    out_rows = (hidden_one + ffn_normed).astype(jnp.bfloat16)
    grad_rows = grad_seq.astype(jnp.float32)
    d_ffn_proj, g_gain_three = rms_backward(ffn_proj, out_scale, norm_gains[3], grad_rows)
    d_ffn_b = d_ffn_proj.astype(jnp.bfloat16)
    grad_down = jnp.dot(mixed_b.T, d_ffn_b, preferred_element_type=jnp.float32)
    d_mixed = jnp.dot(d_ffn_b, w_down.T, preferred_element_type=jnp.float32)
    d_gate_b = (d_mixed * up_proj * gelu_slope(gate_pre)).astype(jnp.bfloat16)
    d_up_b = (d_mixed * activated).astype(jnp.bfloat16)
    grad_gate = jnp.dot(ffn_b.T, d_gate_b, preferred_element_type=jnp.float32)
    grad_up = jnp.dot(ffn_b.T, d_up_b, preferred_element_type=jnp.float32)
    d_ffn_in = jnp.dot(d_gate_b, w_gate.T, preferred_element_type=jnp.float32) + jnp.dot(d_up_b, w_up.T, preferred_element_type=jnp.float32)
    d_hidden_part, g_gain_two = rms_backward(hidden_one, ffn_scale, norm_gains[2], d_ffn_in)
    d_hidden_one = grad_rows + d_hidden_part
    d_attn_proj, g_gain_one = rms_backward(attn_proj, attn_scale, norm_gains[1], d_hidden_one)
    d_attn_b = d_attn_proj.astype(jnp.bfloat16)
    grad_out = jnp.dot(attn_b.T, d_attn_b, preferred_element_type=jnp.float32)
    d_heads = jnp.dot(d_attn_b, w_out.T, preferred_element_type=jnp.float32).astype(jnp.bfloat16).reshape(length, HQ, HD)
    attn_heads = attn_b.reshape(length, HQ, HD)
    row_delta = lax.optimization_barrier(jnp.sum(d_heads.astype(jnp.float32) * attn_heads.astype(jnp.float32), axis=-1))
    delta_blocks = row_delta.reshape(blocks, block_rows, HQ)
    dout_blocks = d_heads.reshape(blocks, block_rows, HQ, HD)

    def backward_block(running, operands):
        key_acc, value_acc = running
        query_blk, pos_blk, lse_blk, dout_blk, delta_blk = operands
        scores, causal = score_block(query_blk, k_rot, pos_blk, positions)
        attn_probs = jnp.where(causal, jnp.exp(scores - lse_blk[..., None]), 0.0).astype(jnp.bfloat16)
        probs_f = attn_probs.astype(jnp.float32)
        dout_f = dout_blk.astype(jnp.float32)
        d_probs = jnp.einsum('thd,sd->hts', dout_f, v_rows.astype(jnp.float32))
        d_scores = (probs_f * (d_probs - jnp.transpose(delta_blk)[:, :, None])).astype(jnp.bfloat16)
        dscore_f = d_scores.astype(jnp.float32)
        value_acc = value_acc + jnp.einsum('hts,thd->sd', probs_f, dout_f)
        key_acc = key_acc + jnp.einsum('hts,thd->sd', dscore_f, query_blk.astype(jnp.float32))
        d_query = jnp.einsum('hts,sd->thd', dscore_f, k_rot.astype(jnp.float32))
        return ((key_acc, value_acc), d_query)
    zero_rows = jnp.zeros((length, HD), jnp.float32)
    (d_keys, d_values), d_queries = lax.scan(backward_block, (zero_rows, zero_rows), (q_blocks, pos_blocks, log_totals, dout_blocks, delta_blocks))
    d_queries = d_queries.reshape(length, HQ, HD)
    d_q_normed = rotate_back(d_queries * query_scale, cos_tab[:, None, :], sin_tab[:, None, :])
    d_k_normed = rotate_back(d_keys, cos_tab, sin_tab)
    d_query_pre, g_head_query = rms_backward(queries, q_scale, head_gains[0], d_q_normed)
    d_key_pre, g_head_key = rms_backward(key_pre, k_scale, head_gains[1], d_k_normed)
    dq_b = d_query_pre.reshape(length, HQ * HD).astype(jnp.bfloat16)
    dk_b = d_key_pre.astype(jnp.bfloat16)
    dv_b = d_values.astype(jnp.bfloat16)
    grad_query = jnp.dot(normed_b.T, dq_b, preferred_element_type=jnp.float32)
    grad_key = jnp.dot(normed_b.T, dk_b, preferred_element_type=jnp.float32)
    grad_value = jnp.dot(normed_b.T, dv_b, preferred_element_type=jnp.float32)
    d_normed = jnp.dot(dq_b, w_query.T, preferred_element_type=jnp.float32) + jnp.dot(dk_b, w_key.T, preferred_element_type=jnp.float32) + jnp.dot(dv_b, w_value.T, preferred_element_type=jnp.float32)
    d_input_part, g_gain_zero = rms_backward(input_rows, in_scale, norm_gains[0], d_normed)
    d_input = d_hidden_one + d_input_part
    grad_flat = jnp.concatenate([grad_query.reshape(-1), grad_key.reshape(-1), grad_value.reshape(-1), grad_out.reshape(-1), grad_gate.reshape(-1), grad_up.reshape(-1), grad_down.reshape(-1), jnp.stack([g_gain_zero, g_gain_one, g_gain_two, g_gain_three]).reshape(-1), jnp.stack([g_head_query, g_head_key]).reshape(-1)])
    return (out_rows, d_input, grad_flat)

def reference(inputs, cotangent, params, first_moment, second_moment):
    weights = unpack(params.astype(jnp.bfloat16), D, HQ, HD, FF)

    def per_sequence(running, operands):
        input_seq, grad_seq = operands
        out_rows, d_input, grad_flat = sequence_pass(input_seq, grad_seq, weights)
        return (running + grad_flat, (out_rows, d_input))
    grads, (outputs, input_grad) = lax.scan(per_sequence, jnp.zeros((PARAMS,), jnp.float32), (inputs, cotangent))
    squares = jnp.sum(grads * grads)
    clip_scale = jnp.minimum(1.0, lax.rsqrt(squares / PARAMS + 1e-06))
    new_params, new_first, new_second = adam_update(params, first_moment, second_moment, grads, clip_scale)
    return (outputs, input_grad, new_params, new_first, new_second, grads)
```

```python
import functools
import math

import jax
import jax.numpy as jnp
from jax import lax
from jax.experimental import pallas as pl
from jax.experimental.pallas import tpu as pltpu
from jax.sharding import PartitionSpec as P

D = 640
HQ = 4
HD = 256
FF = 2048


norm_eps = 1e-06
rope_base = 1000000.0
beta_one = 0.9
beta_two = 0.999
learn_rate = 0.01
decay_rate = 0.1
adam_eps = 1e-08
adam_step = 3
gelu_coef = 0.7978845608028654


def gelu_value(pre_act):
    tanh_part = jnp.tanh(gelu_coef * (pre_act + 0.044715 * pre_act * pre_act * pre_act))
    return 0.5 * pre_act * (1.0 + tanh_part)


def gelu_slope(pre_act):
    tanh_part = jnp.tanh(gelu_coef * (pre_act + 0.044715 * pre_act * pre_act * pre_act))
    return 0.5 * (1.0 + tanh_part) + 0.5 * pre_act * (1.0 - tanh_part * tanh_part) * gelu_coef * (
        1.0 + 3.0 * 0.044715 * pre_act * pre_act
    )


def rms_forward(values_in, gain_row):
    inv_rms = lax.rsqrt(jnp.mean(values_in * values_in, axis=-1, keepdims=True) + norm_eps)
    return (values_in * inv_rms * (1.0 + gain_row), inv_rms)


def rms_backward(values_in, inv_rms, gain_row, grad_out):
    weighted = grad_out * (1.0 + gain_row)
    grad_in = inv_rms * (
        weighted
        - values_in * inv_rms * inv_rms * jnp.mean(weighted * values_in, axis=-1, keepdims=True)
    )
    leading = tuple(range(values_in.ndim - 1))
    grad_gain = jnp.sum(grad_out * values_in * inv_rms, axis=leading)
    return (grad_in, grad_gain)


def rotary_tables(positions, head_dim):
    half_dim = head_dim // 2
    freqs = jnp.exp(
        jnp.arange(half_dim, dtype=jnp.float32) * (-2.0 * math.log(rope_base) / head_dim)
    )
    angles = positions.astype(jnp.float32)[:, None] * freqs[None, :]
    return (jnp.cos(angles), jnp.sin(angles))


def rotate(tensor, cos_part, sin_part):
    half_dim = tensor.shape[-1] // 2
    first_half = tensor[..., :half_dim]
    second_half = tensor[..., half_dim:]
    return jnp.concatenate(
        [
            first_half * cos_part - second_half * sin_part,
            second_half * cos_part + first_half * sin_part,
        ],
        axis=-1,
    )


def rotate_back(tensor, cos_part, sin_part):
    half_dim = tensor.shape[-1] // 2
    first_half = tensor[..., :half_dim]
    second_half = tensor[..., half_dim:]
    return jnp.concatenate(
        [
            first_half * cos_part + second_half * sin_part,
            second_half * cos_part - first_half * sin_part,
        ],
        axis=-1,
    )


def unpack(flat_values, model_width, head_count, head_dim, hidden):
    layouts = [
        (model_width, head_count * head_dim),
        (model_width, head_dim),
        (model_width, head_dim),
        (head_count * head_dim, model_width),
        (model_width, hidden),
        (model_width, hidden),
        (hidden, model_width),
        (4, model_width),
        (2, head_dim),
    ]
    pieces = []
    offset = 0
    for layout in layouts:
        amount = layout[0] * layout[1]
        pieces.append(flat_values[offset : offset + amount].reshape(layout))
        offset += amount
    return pieces


def adam_update(weights, moment_one, moment_two, grad_values, clip_scale):
    clipped = grad_values * clip_scale
    new_one = beta_one * moment_one + (1.0 - beta_one) * clipped
    new_two = beta_two * moment_two + (1.0 - beta_two) * clipped * clipped
    corrected_one = new_one / (1.0 - beta_one**adam_step)
    corrected_two = new_two / (1.0 - beta_two**adam_step)
    new_weights = weights - learn_rate * (
        corrected_one / (jnp.sqrt(corrected_two) + adam_eps) + decay_rate * weights
    )
    return (new_weights, new_one, new_two)


def clip_factor(squares, amount):
    return jnp.minimum(1.0, lax.rsqrt(squares / amount + 1e-06))


MESH_ID = pl.DeviceIdType.MESH
LANES = 128
VMEM_LIMIT = 60 * 1024 * 1024


def ring(position, step, size):
    return lax.rem(position + step, size)


def back(position, step, size):
    return lax.rem(position + size - step, size)


def greet(peers):
    barrier = pltpu.get_barrier_semaphore()
    for peer in peers:
        pl.semaphore_signal(barrier, inc=1, device_id=peer, device_id_type=MESH_ID)
    pl.semaphore_wait(barrier, len(peers))


def remote(src, dst, send_sem, recv_sem, peer):
    return pltpu.make_async_remote_copy(
        src_ref=src,
        dst_ref=dst,
        send_sem=send_sem,
        recv_sem=recv_sem,
        device_id=peer,
        device_id_type=MESH_ID,
    )


def gather_kernel(
    nd, nc, nz, x_ref, full_ref, own_sem, s1s, s1r, s2s, s2r, s3s, s3r, sos, sor
):
    d = lax.axis_index("dp")
    c = lax.axis_index("ctx")
    z = lax.axis_index("zero")
    greet(
        [{"zero": ring(z, k, nz)} for k in range(1, nz)]
        + [{"dp": ring(d, i, nd)} for i in range(1, nd)]
        + [{"ctx": ring(c, j, nc)} for j in range(1, nc)]
    )
    sends = []

    def start(src, dst, ssem, rsem, peer):
        copy = remote(src, dst, ssem, rsem, peer)
        copy.start()
        sends.append(copy)

    for k in range(1, nz):
        start(
            x_ref.at[d], full_ref.at[c, z, d], s1s.at[k], s1r.at[k], {"zero": ring(z, k, nz)}
        )
    own = pltpu.make_async_copy(x_ref, full_ref.at[c, z], own_sem)
    own.start()
    for j in range(1, nc):
        start(x_ref, full_ref.at[c, z], sos.at[j], sor.at[j], {"ctx": ring(c, j, nc)})

    def arrived(ref, sem, peer):
        remote(ref, ref, s1s.at[0], sem, peer).wait_recv()

    for k in range(1, nz):
        src_z = back(z, k, nz)
        piece = full_ref.at[c, src_z, d]
        arrived(piece, s1r.at[k], {"zero": ring(z, k, nz)})
        for i in range(1, nd):
            start(piece, piece, s2s.at[k, i], s2r.at[k, i], {"dp": ring(d, i, nd)})
        for j in range(1, nc):
            start(piece, piece, s3s.at[k, 0, j], s3r.at[k, 0, j], {"ctx": ring(c, j, nc)})
    for k in range(1, nz):
        src_z = back(z, k, nz)
        for i in range(1, nd):
            piece = full_ref.at[c, src_z, back(d, i, nd)]
            arrived(piece, s2r.at[k, i], {"dp": ring(d, i, nd)})
            for j in range(1, nc):
                start(piece, piece, s3s.at[k, i, j], s3r.at[k, i, j], {"ctx": ring(c, j, nc)})
    for j in range(1, nc):
        src_c = back(c, j, nc)
        peer = {"ctx": ring(c, j, nc)}
        arrived(full_ref.at[src_c, z], sor.at[j], peer)
        for k in range(1, nz):
            for i in range(nd):
                arrived(
                    full_ref.at[src_c, back(z, k, nz), back(d, i, nd)], s3r.at[k, i, j], peer
                )
    for copy in sends:
        copy.wait_send()
    own.wait()


def gather_weights(x, nd, nc, nz):
    dma = pltpu.SemaphoreType.DMA
    return pl.pallas_call(
        functools.partial(gather_kernel, nd, nc, nz),
        out_shape=jax.ShapeDtypeStruct((nc, nz) + x.shape, x.dtype),
        in_specs=[pl.BlockSpec(memory_space=pltpu.VMEM)],
        out_specs=pl.BlockSpec(memory_space=pl.ANY),
        scratch_shapes=[
            dma,
            dma((nz,)),
            dma((nz,)),
            dma((nz, nd)),
            dma((nz, nd)),
            dma((nz, nd, nc)),
            dma((nz, nd, nc)),
            dma((nc,)),
            dma((nc,)),
        ],
        compiler_params=pltpu.CompilerParams(
            collective_id=0, has_side_effects=True, vmem_limit_bytes=VMEM_LIMIT
        ),
        name="gather_weights",
    )(x)


def reduce_kernel(
    nd, nc, nz, rows, g_ref, out_ref, sq_ref,
    a_buf, b_src, b_buf, c_src, c_buf, d_buf,
    sas, sar, sbs, sbr, scs, scr, sds, sdr, sqs, sqr,
):
    d = lax.axis_index("dp")
    c = lax.axis_index("ctx")
    z = lax.axis_index("zero")
    step_rows = 32
    greet(
        [
            {"ctx": ring(c, j, nc), "zero": ring(z, k, nz)}
            for j in range(nc)
            for k in range(nz)
            if j or k
        ]
        + [{"dp": ring(d, i, nd)} for i in range(1, nd)]
    )
    sends = []

    def start(src, dst, ssem, rsem, peer):
        copy = remote(src, dst, ssem, rsem, peer)
        copy.start()
        sends.append(copy)
        return copy

    first = []
    for k in range(nz):
        dst_z = ring(z, k + 1, nz)
        first.append(
            [
                start(
                    g_ref.at[ring(c, j, nc), dst_z],
                    a_buf.at[k, j - 1],
                    sas.at[k, j],
                    sar.at[k, j],
                    {"ctx": ring(c, j, nc)},
                )
                for j in range(1, nc)
            ]
        )
    second = []
    for k in range(nz):
        dst_z = ring(z, k + 1, nz)
        for copy in first[k]:
            copy.wait_recv()

        def add_ctx(r, carry, k=k, dst_z=dst_z):
            at = pl.ds(pl.multiple_of(r * step_rows, step_rows), step_rows)
            total = g_ref[c, dst_z, :, at, :].astype(jnp.float32)
            for j in range(1, nc):
                total = total + a_buf[k, j - 1, :, at, :].astype(jnp.float32)
            b_src[k, :, at, :] = total.astype(jnp.bfloat16)
            return carry

        lax.fori_loop(0, rows // step_rows, add_ctx, 0)
        second.append(
            [
                start(
                    b_src.at[k, ring(d, i, nd)],
                    b_buf.at[k, i - 1],
                    sbs.at[k, i],
                    sbr.at[k, i],
                    {"dp": ring(d, i, nd)},
                )
                for i in range(1, nd)
            ]
        )
    third = []
    for k in range(nz):
        for copy in second[k]:
            copy.wait_recv()

        def add_dp(r, carry, k=k):
            at = pl.ds(pl.multiple_of(r * step_rows, step_rows), step_rows)
            total = b_src[k, d, at, :].astype(jnp.float32)
            for i in range(1, nd):
                total = total + b_buf[k, i - 1, at, :].astype(jnp.float32)
            c_src[k, at, :] = total.astype(jnp.bfloat16)
            return carry

        lax.fori_loop(0, rows // step_rows, add_dp, 0)
        if k < nz - 1:
            third.append(
                start(
                    c_src.at[k],
                    c_buf.at[k],
                    scs.at[k],
                    scr.at[k],
                    {"zero": ring(z, k + 1, nz)},
                )
            )
    for copy in third:
        copy.wait_recv()

    def add_zero(r, carry):
        at = pl.ds(pl.multiple_of(r * step_rows, step_rows), step_rows)
        total = c_src[nz - 1, at, :].astype(jnp.float32)
        for k in range(nz - 1):
            total = total + c_buf[k, at, :].astype(jnp.float32)
        d_buf[d, at, :] = total.astype(jnp.bfloat16)
        return carry

    lax.fori_loop(0, rows // step_rows, add_zero, 0)
    mine = d_buf.at[d]
    for i in range(1, nd):
        start(mine, mine, sds.at[i], sdr.at[i], {"dp": ring(d, i, nd)})
    for i in range(1, nd):
        theirs = d_buf.at[back(d, i, nd)]
        remote(theirs, theirs, sds.at[i], sdr.at[i], {"dp": ring(d, i, nd)}).wait_recv()

    def finish(r, carry):
        at = pl.ds(pl.multiple_of(r * step_rows, step_rows), step_rows)
        total = d_buf[:, at, :].astype(jnp.float32)
        out_ref[:, at, :] = total
        return carry + jnp.sum((total * total).reshape(-1, 8, LANES), axis=0)

    sq_ref[0] = lax.fori_loop(
        0, rows // step_rows, finish, jnp.zeros((8, LANES), jnp.float32)
    )
    last = []
    for j in range(nc):
        for k in range(nz):
            slot = j * nz + k
            if slot:
                last.append(
                    start(
                        sq_ref.at[0],
                        sq_ref.at[slot],
                        sqs.at[slot],
                        sqr.at[slot],
                        {"ctx": ring(c, j, nc), "zero": ring(z, k, nz)},
                    )
                )
    for copy in last:
        copy.wait_recv()
    for copy in sends:
        copy.wait_send()


def reduce_grads(g, nd, nc, nz):
    dma = pltpu.SemaphoreType.DMA
    rows = g.shape[3]
    vmem = pl.BlockSpec(memory_space=pltpu.VMEM)
    return pl.pallas_call(
        functools.partial(reduce_kernel, nd, nc, nz, rows),
        out_shape=(
            jax.ShapeDtypeStruct((nd, rows, LANES), jnp.float32),
            jax.ShapeDtypeStruct((nc * nz, 8, LANES), jnp.float32),
        ),
        in_specs=[vmem],
        out_specs=(vmem, vmem),
        scratch_shapes=[
            pltpu.VMEM((nz, max(nc - 1, 1), nd, rows, LANES), jnp.bfloat16),
            pltpu.VMEM((nz, nd, rows, LANES), jnp.bfloat16),
            pltpu.VMEM((nz, max(nd - 1, 1), rows, LANES), jnp.bfloat16),
            pltpu.VMEM((nz, rows, LANES), jnp.bfloat16),
            pltpu.VMEM((nz, rows, LANES), jnp.bfloat16),
            pltpu.VMEM((nd, rows, LANES), jnp.bfloat16),
            dma((nz, nc)),
            dma((nz, nc)),
            dma((nz, nd)),
            dma((nz, nd)),
            dma((nz,)),
            dma((nz,)),
            dma((nd,)),
            dma((nd,)),
            dma((nc * nz,)),
            dma((nc * nz,)),
        ],
        compiler_params=pltpu.CompilerParams(
            collective_id=1, has_side_effects=True, vmem_limit_bytes=VMEM_LIMIT
        ),
        name="reduce_grads",
    )(g)


def share_kernel(nc, x_ref, out_ref, buf, own_sem, ssem, rsem):
    c = lax.axis_index("ctx")
    greet([{"ctx": ring(c, j, nc)} for j in range(1, nc)])
    copies = []
    for j in range(1, nc):
        copy = remote(x_ref, buf.at[j - 1], ssem.at[j], rsem.at[j], {"ctx": ring(c, j, nc)})
        copy.start()
        copies.append(copy)
    out_ref[c] = x_ref[...]
    for j in range(1, nc):
        copies[j - 1].wait()
        out_ref[back(c, j, nc)] = buf[j - 1]


def share_rows(x, nc):
    dma = pltpu.SemaphoreType.DMA
    vmem = pl.BlockSpec(memory_space=pltpu.VMEM)
    return pl.pallas_call(
        functools.partial(share_kernel, nc),
        out_shape=jax.ShapeDtypeStruct((nc,) + x.shape, x.dtype),
        in_specs=[vmem],
        out_specs=vmem,
        scratch_shapes=[
            pltpu.VMEM((max(nc - 1, 1),) + x.shape, x.dtype),
            dma,
            dma((nc,)),
            dma((nc,)),
        ],
        compiler_params=pltpu.CompilerParams(collective_id=2, has_side_effects=True),
        name="share_rows",
    )(x)


def sum_kernel(nc, x_ref, out_ref, buf, ssem, rsem):
    c = lax.axis_index("ctx")
    greet([{"ctx": ring(c, j, nc)} for j in range(1, nc)])
    copies = []
    for j in range(1, nc):
        copy = remote(
            x_ref.at[ring(c, j, nc)],
            buf.at[j - 1],
            ssem.at[j],
            rsem.at[j],
            {"ctx": ring(c, j, nc)},
        )
        copy.start()
        copies.append(copy)
    total = x_ref[c]
    for j in range(1, nc):
        copies[j - 1].wait()
        total = total + buf[j - 1]
    out_ref[...] = total


def sum_rows(x, nc):
    dma = pltpu.SemaphoreType.DMA
    vmem = pl.BlockSpec(memory_space=pltpu.VMEM)
    return pl.pallas_call(
        functools.partial(sum_kernel, nc),
        out_shape=jax.ShapeDtypeStruct(x.shape[1:], x.dtype),
        in_specs=[vmem],
        out_specs=vmem,
        scratch_shapes=[
            pltpu.VMEM((max(nc - 1, 1),) + x.shape[1:], x.dtype),
            dma((nc,)),
            dma((nc,)),
        ],
        compiler_params=pltpu.CompilerParams(collective_id=3, has_side_effects=True),
        name="sum_rows",
    )(x)


def quarter_rows(shard_size, nd):
    return -(-shard_size // (nd * LANES * 32)) * 32


def pack_shards(flat, shards, nd, rows):
    per_shard = flat.reshape(shards, -1)
    pad = nd * rows * LANES - per_shard.shape[1]
    return jnp.pad(per_shard, ((0, 0), (0, pad)))


def local(sizes, inputs, cotangent, params, first_moment, second_moment):
    tokens = inputs.shape[1]
    nd, nc, nz = sizes
    shard = params.shape[0]
    rows = quarter_rows(shard, nd)
    own_b = pack_shards(params.astype(jnp.bfloat16), 1, nd, rows).reshape(nd, rows, LANES)
    gathered = gather_weights(own_b, nd, nc, nz)
    gathered = gathered.reshape(nc * nz, -1)[:, :shard].reshape(-1)
    w_query, w_key, w_value, w_out, w_gate, w_up, w_down, norm_gains, head_gains = unpack(
        gathered, D, HQ, HD, FF
    )
    norm_gains = norm_gains.astype(jnp.float32)
    head_gains = head_gains.astype(jnp.float32)
    positions = lax.axis_index("ctx") * tokens + jnp.arange(tokens, dtype=jnp.int32)
    cos_tab, sin_tab = rotary_tables(positions, HD)
    input_rows = inputs[0].astype(jnp.float32)
    normed_in, in_scale = rms_forward(input_rows, norm_gains[0])
    normed_b = normed_in.astype(jnp.bfloat16)
    queries = jnp.dot(normed_b, w_query, preferred_element_type=jnp.float32).reshape(tokens, HQ, HD)
    key_pre = jnp.dot(normed_b, w_key, preferred_element_type=jnp.float32)
    values = jnp.dot(normed_b, w_value, preferred_element_type=jnp.float32)
    q_normed, q_scale = rms_forward(queries, head_gains[0])
    k_normed, k_scale = rms_forward(key_pre, head_gains[1])
    query_scale = HD ** (-0.5)
    q_rot = (rotate(q_normed, cos_tab[:, None, :], sin_tab[:, None, :]) * query_scale).astype(
        jnp.bfloat16
    )
    k_rot = rotate(k_normed, cos_tab, sin_tab).astype(jnp.bfloat16)
    v_rows = values.astype(jnp.bfloat16)
    shared = share_rows(jnp.concatenate([k_rot, v_rows], axis=1), nc).reshape(nc * tokens, 2 * HD)
    all_keys, all_values = shared[:, :HD], shared[:, HD:]
    length = all_keys.shape[0]
    key_pos = jnp.arange(length, dtype=jnp.int32)
    block_rows = math.gcd(tokens, 512)
    blocks = tokens // block_rows
    q_blocks = q_rot.reshape(blocks, block_rows, HQ, HD)
    pos_blocks = positions.reshape(blocks, block_rows)

    def score_block(query_blk, pos_blk):
        scores = jnp.einsum("thd,sd->hts", query_blk, all_keys, preferred_element_type=jnp.float32)
        causal = key_pos[None, None, :] <= pos_blk[None, :, None]
        return (scores, causal)

    def forward_block(operands):
        query_blk, pos_blk = operands
        scores, causal = score_block(query_blk, pos_blk)
        row_total = jnp.sum(jnp.where(causal, jnp.exp(scores), 0.0), axis=-1)
        log_total = jnp.log(row_total)
        attn_probs = jnp.where(causal, jnp.exp(scores - log_total[..., None]), 0.0).astype(
            jnp.bfloat16
        )
        attended = jnp.einsum(
            "hts,sd->thd", attn_probs, all_values, preferred_element_type=jnp.float32
        )
        return (attended, log_total)

    attended, log_totals = lax.map(forward_block, (q_blocks, pos_blocks))
    attn_b = attended.reshape(tokens, HQ * HD).astype(jnp.bfloat16)
    attn_proj = jnp.dot(attn_b, w_out, preferred_element_type=jnp.float32)
    attn_normed, attn_scale = rms_forward(attn_proj, norm_gains[1])
    hidden_one = input_rows + attn_normed
    ffn_in, ffn_scale = rms_forward(hidden_one, norm_gains[2])
    ffn_b = ffn_in.astype(jnp.bfloat16)
    gate_pre = jnp.dot(ffn_b, w_gate, preferred_element_type=jnp.float32)
    up_proj = jnp.dot(ffn_b, w_up, preferred_element_type=jnp.float32)
    activated = gelu_value(gate_pre)
    mixed_b = (activated * up_proj).astype(jnp.bfloat16)
    ffn_proj = jnp.dot(mixed_b, w_down, preferred_element_type=jnp.float32)
    ffn_normed, out_scale = rms_forward(ffn_proj, norm_gains[3])
    out_rows = (hidden_one + ffn_normed).astype(jnp.bfloat16)
    grad_rows = cotangent[0].astype(jnp.float32)
    d_ffn_proj, g_gain_three = rms_backward(ffn_proj, out_scale, norm_gains[3], grad_rows)
    d_ffn_b = d_ffn_proj.astype(jnp.bfloat16)
    grad_down = jnp.dot(mixed_b.T, d_ffn_b, preferred_element_type=jnp.float32)
    d_mixed = jnp.dot(d_ffn_b, w_down.T, preferred_element_type=jnp.float32)
    d_gate_b = (d_mixed * up_proj * gelu_slope(gate_pre)).astype(jnp.bfloat16)
    d_up_b = (d_mixed * activated).astype(jnp.bfloat16)
    grad_gate = jnp.dot(ffn_b.T, d_gate_b, preferred_element_type=jnp.float32)
    grad_up = jnp.dot(ffn_b.T, d_up_b, preferred_element_type=jnp.float32)
    d_ffn_in = jnp.dot(d_gate_b, w_gate.T, preferred_element_type=jnp.float32) + jnp.dot(
        d_up_b, w_up.T, preferred_element_type=jnp.float32
    )
    d_hidden_part, g_gain_two = rms_backward(hidden_one, ffn_scale, norm_gains[2], d_ffn_in)
    d_hidden_one = grad_rows + d_hidden_part
    d_attn_proj, g_gain_one = rms_backward(attn_proj, attn_scale, norm_gains[1], d_hidden_one)
    d_attn_b = d_attn_proj.astype(jnp.bfloat16)
    grad_out = jnp.dot(attn_b.T, d_attn_b, preferred_element_type=jnp.float32)
    d_heads = (
        jnp.dot(d_attn_b, w_out.T, preferred_element_type=jnp.float32)
        .astype(jnp.bfloat16)
        .reshape(tokens, HQ, HD)
    )
    attn_heads = attn_b.reshape(tokens, HQ, HD)
    row_delta = jnp.sum(d_heads.astype(jnp.float32) * attn_heads.astype(jnp.float32), axis=-1)
    delta_blocks = row_delta.reshape(blocks, block_rows, HQ)
    dout_blocks = d_heads.reshape(blocks, block_rows, HQ, HD)

    def backward_block(running, operands):
        key_acc, value_acc = running
        query_blk, pos_blk, lse_blk, dout_blk, delta_blk = operands
        scores, causal = score_block(query_blk, pos_blk)
        attn_probs = jnp.where(causal, jnp.exp(scores - lse_blk[..., None]), 0.0).astype(
            jnp.bfloat16
        )
        d_probs = jnp.einsum(
            "thd,sd->hts", dout_blk, all_values, preferred_element_type=jnp.float32
        )
        d_scores = (
            attn_probs.astype(jnp.float32) * (d_probs - jnp.transpose(delta_blk)[:, :, None])
        ).astype(jnp.bfloat16)
        value_acc = value_acc + jnp.einsum(
            "hts,thd->sd", attn_probs, dout_blk, preferred_element_type=jnp.float32
        )
        key_acc = key_acc + jnp.einsum(
            "hts,thd->sd", d_scores, query_blk, preferred_element_type=jnp.float32
        )
        d_query = jnp.einsum("hts,sd->thd", d_scores, all_keys, preferred_element_type=jnp.float32)
        return ((key_acc, value_acc), d_query)

    zero_rows = jnp.zeros((length, HD), jnp.float32)
    (key_terms, value_terms), d_queries = lax.scan(
        backward_block,
        (zero_rows, zero_rows),
        (q_blocks, pos_blocks, log_totals, dout_blocks, delta_blocks),
    )
    d_both = sum_rows(
        jnp.concatenate([key_terms, value_terms], axis=1).reshape(nc, tokens, 2 * HD), nc
    )
    d_keys, d_values = d_both[:, :HD], d_both[:, HD:]
    d_queries = d_queries.reshape(tokens, HQ, HD)
    d_q_normed = rotate_back(d_queries * query_scale, cos_tab[:, None, :], sin_tab[:, None, :])
    d_k_normed = rotate_back(d_keys, cos_tab, sin_tab)
    d_query_pre, g_head_query = rms_backward(queries, q_scale, head_gains[0], d_q_normed)
    d_key_pre, g_head_key = rms_backward(key_pre, k_scale, head_gains[1], d_k_normed)
    dq_b = d_query_pre.reshape(tokens, HQ * HD).astype(jnp.bfloat16)
    dk_b = d_key_pre.astype(jnp.bfloat16)
    dv_b = d_values.astype(jnp.bfloat16)
    grad_query = jnp.dot(normed_b.T, dq_b, preferred_element_type=jnp.float32)
    grad_key = jnp.dot(normed_b.T, dk_b, preferred_element_type=jnp.float32)
    grad_value = jnp.dot(normed_b.T, dv_b, preferred_element_type=jnp.float32)
    d_normed = (
        jnp.dot(dq_b, w_query.T, preferred_element_type=jnp.float32)
        + jnp.dot(dk_b, w_key.T, preferred_element_type=jnp.float32)
        + jnp.dot(dv_b, w_value.T, preferred_element_type=jnp.float32)
    )
    d_input_part, g_gain_zero = rms_backward(input_rows, in_scale, norm_gains[0], d_normed)
    d_input = (d_hidden_one + d_input_part)[None]
    flat_grad = jnp.concatenate(
        [
            grad_query.reshape(-1),
            grad_key.reshape(-1),
            grad_value.reshape(-1),
            grad_out.reshape(-1),
            grad_gate.reshape(-1),
            grad_up.reshape(-1),
            grad_down.reshape(-1),
            jnp.stack([g_gain_zero, g_gain_one, g_gain_two, g_gain_three]).reshape(-1),
            jnp.stack([g_head_query, g_head_key]).reshape(-1),
        ]
    )
    total_params = flat_grad.shape[0]
    packed = pack_shards(flat_grad.astype(jnp.bfloat16), nc * nz, nd, rows)
    summed, square_parts = reduce_grads(packed.reshape(nc, nz, nd, rows, LANES), nd, nc, nz)
    summed = summed.reshape(-1)[:shard]
    squares = jnp.sum(square_parts)
    new_params, new_first, new_second = adam_update(
        params, first_moment, second_moment, summed, clip_factor(squares, total_params)
    )
    return (out_rows[None], d_input, new_params, new_first, new_second, summed)


def solution(mesh):
    sizes = tuple(mesh.shape[axis] for axis in ("dp", "ctx", "zero"))
    placed = (
        P(("dp", "zero"), "ctx", None),
        P(("dp", "zero"), "ctx", None),
        P(("ctx", "zero")),
        P(("ctx", "zero")),
        P(("ctx", "zero")),
    )
    return jax.shard_map(
        functools.partial(local, sizes),
        mesh=mesh,
        in_specs=placed,
        out_specs=(
            P(("dp", "zero"), "ctx", None),
            P(("dp", "zero"), "ctx", None),
            P(("ctx", "zero")),
            P(("ctx", "zero")),
            P(("ctx", "zero")),
            P(("ctx", "zero")),
        ),
        check_vma=False,
    )
```

```python
import functools
import math

import jax
import jax.numpy as jnp
from jax import lax
from jax.experimental import pallas as pl
from jax.experimental.pallas import tpu as pltpu
from jax.sharding import PartitionSpec as P

D = 640
HQ = 4
HD = 256
FF = 2048


norm_eps = 1e-06
rope_base = 1000000.0
beta_one = 0.9
beta_two = 0.999
learn_rate = 0.01
decay_rate = 0.1
adam_eps = 1e-08
adam_step = 3
gelu_coef = 0.7978845608028654


def gelu_value(pre_act):
    tanh_part = jnp.tanh(gelu_coef * (pre_act + 0.044715 * pre_act * pre_act * pre_act))
    return 0.5 * pre_act * (1.0 + tanh_part)


def gelu_slope(pre_act):
    tanh_part = jnp.tanh(gelu_coef * (pre_act + 0.044715 * pre_act * pre_act * pre_act))
    return 0.5 * (1.0 + tanh_part) + 0.5 * pre_act * (1.0 - tanh_part * tanh_part) * gelu_coef * (
        1.0 + 3.0 * 0.044715 * pre_act * pre_act
    )


def rms_forward(values_in, gain_row):
    inv_rms = lax.rsqrt(jnp.mean(values_in * values_in, axis=-1, keepdims=True) + norm_eps)
    return (values_in * inv_rms * (1.0 + gain_row), inv_rms)


def rms_backward(values_in, inv_rms, gain_row, grad_out):
    weighted = grad_out * (1.0 + gain_row)
    grad_in = inv_rms * (
        weighted
        - values_in * inv_rms * inv_rms * jnp.mean(weighted * values_in, axis=-1, keepdims=True)
    )
    leading = tuple(range(values_in.ndim - 1))
    grad_gain = jnp.sum(grad_out * values_in * inv_rms, axis=leading)
    return (grad_in, grad_gain)


def rotary_tables(positions, head_dim):
    half_dim = head_dim // 2
    freqs = jnp.exp(
        jnp.arange(half_dim, dtype=jnp.float32) * (-2.0 * math.log(rope_base) / head_dim)
    )
    angles = positions.astype(jnp.float32)[:, None] * freqs[None, :]
    return (jnp.cos(angles), jnp.sin(angles))


def rotate(tensor, cos_part, sin_part):
    half_dim = tensor.shape[-1] // 2
    first_half = tensor[..., :half_dim]
    second_half = tensor[..., half_dim:]
    return jnp.concatenate(
        [
            first_half * cos_part - second_half * sin_part,
            second_half * cos_part + first_half * sin_part,
        ],
        axis=-1,
    )


def rotate_back(tensor, cos_part, sin_part):
    half_dim = tensor.shape[-1] // 2
    first_half = tensor[..., :half_dim]
    second_half = tensor[..., half_dim:]
    return jnp.concatenate(
        [
            first_half * cos_part + second_half * sin_part,
            second_half * cos_part - first_half * sin_part,
        ],
        axis=-1,
    )


def unpack(flat_values, model_width, head_count, head_dim, hidden):
    layouts = [
        (model_width, head_count * head_dim),
        (model_width, head_dim),
        (model_width, head_dim),
        (head_count * head_dim, model_width),
        (model_width, hidden),
        (model_width, hidden),
        (hidden, model_width),
        (4, model_width),
        (2, head_dim),
    ]
    pieces = []
    offset = 0
    for layout in layouts:
        amount = layout[0] * layout[1]
        pieces.append(flat_values[offset : offset + amount].reshape(layout))
        offset += amount
    return pieces


def adam_update(weights, moment_one, moment_two, grad_values, clip_scale):
    clipped = grad_values * clip_scale
    new_one = beta_one * moment_one + (1.0 - beta_one) * clipped
    new_two = beta_two * moment_two + (1.0 - beta_two) * clipped * clipped
    corrected_one = new_one / (1.0 - beta_one**adam_step)
    corrected_two = new_two / (1.0 - beta_two**adam_step)
    new_weights = weights - learn_rate * (
        corrected_one / (jnp.sqrt(corrected_two) + adam_eps) + decay_rate * weights
    )
    return (new_weights, new_one, new_two)


def clip_factor(squares, amount):
    return jnp.minimum(1.0, lax.rsqrt(squares / amount + 1e-06))


MESH_ID = pl.DeviceIdType.MESH
LANES = 128
VMEM_LIMIT = 60 * 1024 * 1024


def ring(position, step, size):
    return lax.rem(position + step, size)


def back(position, step, size):
    return lax.rem(position + size - step, size)


def greet(peers):
    barrier = pltpu.get_barrier_semaphore()
    for peer in peers:
        pl.semaphore_signal(barrier, inc=1, device_id=peer, device_id_type=MESH_ID)
    pl.semaphore_wait(barrier, len(peers))


def remote(src, dst, send_sem, recv_sem, peer):
    return pltpu.make_async_remote_copy(
        src_ref=src,
        dst_ref=dst,
        send_sem=send_sem,
        recv_sem=recv_sem,
        device_id=peer,
        device_id_type=MESH_ID,
    )


def gather_kernel(
    nd, nc, nz, x_ref, full_ref, own_sem, s1s, s1r, s2s, s2r, s3s, s3r, sos, sor
):
    d = lax.axis_index("dp")
    c = lax.axis_index("ctx")
    z = lax.axis_index("zero")
    greet(
        [{"zero": ring(z, k, nz)} for k in range(1, nz)]
        + [{"dp": ring(d, i, nd)} for i in range(1, nd)]
        + [{"ctx": ring(c, j, nc)} for j in range(1, nc)]
    )
    sends = []

    def start(src, dst, ssem, rsem, peer):
        copy = remote(src, dst, ssem, rsem, peer)
        copy.start()
        sends.append(copy)

    for k in range(1, nz):
        start(
            x_ref.at[d], full_ref.at[c, z, d], s1s.at[k], s1r.at[k], {"zero": ring(z, k, nz)}
        )
    own = pltpu.make_async_copy(x_ref, full_ref.at[c, z], own_sem)
    own.start()
    for j in range(1, nc):
        start(x_ref, full_ref.at[c, z], sos.at[j], sor.at[j], {"ctx": ring(c, j, nc)})

    def arrived(ref, sem, peer):
        remote(ref, ref, s1s.at[0], sem, peer).wait_recv()

    for k in range(1, nz):
        src_z = back(z, k, nz)
        piece = full_ref.at[c, src_z, d]
        arrived(piece, s1r.at[k], {"zero": ring(z, k, nz)})
        for i in range(1, nd):
            start(piece, piece, s2s.at[k, i], s2r.at[k, i], {"dp": ring(d, i, nd)})
        for j in range(1, nc):
            start(piece, piece, s3s.at[k, 0, j], s3r.at[k, 0, j], {"ctx": ring(c, j, nc)})
    for k in range(1, nz):
        src_z = back(z, k, nz)
        for i in range(1, nd):
            piece = full_ref.at[c, src_z, back(d, i, nd)]
            arrived(piece, s2r.at[k, i], {"dp": ring(d, i, nd)})
            for j in range(1, nc):
                start(piece, piece, s3s.at[k, i, j], s3r.at[k, i, j], {"ctx": ring(c, j, nc)})
    for j in range(1, nc):
        src_c = back(c, j, nc)
        peer = {"ctx": ring(c, j, nc)}
        arrived(full_ref.at[src_c, z], sor.at[j], peer)
        for k in range(1, nz):
            for i in range(nd):
                arrived(
                    full_ref.at[src_c, back(z, k, nz), back(d, i, nd)], s3r.at[k, i, j], peer
                )
    for copy in sends:
        copy.wait_send()
    own.wait()


def gather_weights(x, nd, nc, nz):
    dma = pltpu.SemaphoreType.DMA
    return pl.pallas_call(
        functools.partial(gather_kernel, nd, nc, nz),
        out_shape=jax.ShapeDtypeStruct((nc, nz) + x.shape, x.dtype),
        in_specs=[pl.BlockSpec(memory_space=pltpu.VMEM)],
        out_specs=pl.BlockSpec(memory_space=pl.ANY),
        scratch_shapes=[
            dma,
            dma((nz,)),
            dma((nz,)),
            dma((nz, nd)),
            dma((nz, nd)),
            dma((nz, nd, nc)),
            dma((nz, nd, nc)),
            dma((nc,)),
            dma((nc,)),
        ],
        compiler_params=pltpu.CompilerParams(
            collective_id=0, has_side_effects=True, vmem_limit_bytes=VMEM_LIMIT
        ),
        name="gather_weights",
    )(x)


def reduce_kernel(
    nd, nc, nz, layout, g_ref, out_ref, sq_ref,
    a_buf, b_src, b_buf, c_src, c_buf, d_buf,
    sas, sar, sbs, sbr, scs, scr, sds, sdr, sqs, sqr,
):
    d = lax.axis_index("dp")
    c = lax.axis_index("ctx")
    z = lax.axis_index("zero")
    step_rows = 32
    rows = layout.part

    def base(col, row):
        return pl.multiple_of(layout.base(col * nz + row), ALIGN)

    greet(
        [
            {"ctx": ring(c, j, nc), "zero": ring(z, k, nz)}
            for j in range(nc)
            for k in range(nz)
            if j or k
        ]
        + [{"dp": ring(d, i, nd)} for i in range(1, nd)]
    )
    sends = []

    def start(src, dst, ssem, rsem, peer):
        copy = remote(src, dst, ssem, rsem, peer)
        copy.start()
        sends.append(copy)
        return copy

    first = []
    for k in range(nz):
        dst_z = ring(z, k + 1, nz)
        first.append(
            [
                start(
                    g_ref.at[pl.ds(base(ring(c, j, nc), dst_z), layout.padded)],
                    a_buf.at[k, j - 1],
                    sas.at[k, j],
                    sar.at[k, j],
                    {"ctx": ring(c, j, nc)},
                )
                for j in range(1, nc)
            ]
        )
    second = []
    for k in range(nz):
        dst_z = ring(z, k + 1, nz)
        for copy in first[k]:
            copy.wait_recv()

        def add_ctx(r, carry, k=k, dst_z=dst_z):
            at = pl.ds(pl.multiple_of(r * step_rows, step_rows), step_rows)
            mine = pl.ds(pl.multiple_of(base(c, dst_z) + r * step_rows, ALIGN), step_rows)
            total = g_ref[mine, :].astype(jnp.float32)
            for j in range(1, nc):
                total = total + a_buf[k, j - 1, at, :].astype(jnp.float32)
            b_src[k, at, :] = total.astype(jnp.bfloat16)
            return carry

        lax.fori_loop(0, layout.padded // step_rows, add_ctx, 0, unroll=4)
        second.append(
            [
                start(
                    b_src.at[k, pl.ds(pl.multiple_of(ring(d, i, nd) * rows, 32), rows)],
                    b_buf.at[k, i - 1],
                    sbs.at[k, i],
                    sbr.at[k, i],
                    {"dp": ring(d, i, nd)},
                )
                for i in range(1, nd)
            ]
        )
    third = []
    for k in range(nz):
        for copy in second[k]:
            copy.wait_recv()

        def add_dp(r, carry, k=k):
            at = pl.ds(pl.multiple_of(r * step_rows, step_rows), step_rows)
            mine = pl.ds(pl.multiple_of(d * rows + r * step_rows, step_rows), step_rows)
            total = b_src[k, mine, :].astype(jnp.float32)
            for i in range(1, nd):
                total = total + b_buf[k, i - 1, at, :].astype(jnp.float32)
            c_src[k, at, :] = total.astype(jnp.bfloat16)
            return carry

        lax.fori_loop(0, rows // step_rows, add_dp, 0)
        if k < nz - 1:
            third.append(
                start(
                    c_src.at[k],
                    c_buf.at[k],
                    scs.at[k],
                    scr.at[k],
                    {"zero": ring(z, k + 1, nz)},
                )
            )
    for copy in third:
        copy.wait_recv()

    def add_zero(r, carry):
        at = pl.ds(pl.multiple_of(r * step_rows, step_rows), step_rows)
        total = c_src[nz - 1, at, :].astype(jnp.float32)
        for k in range(nz - 1):
            total = total + c_buf[k, at, :].astype(jnp.float32)
        d_buf[d, at, :] = total.astype(jnp.bfloat16)
        return carry

    lax.fori_loop(0, rows // step_rows, add_zero, 0)
    mine = d_buf.at[d]
    for i in range(1, nd):
        start(mine, mine, sds.at[i], sdr.at[i], {"dp": ring(d, i, nd)})
    for i in range(1, nd):
        theirs = d_buf.at[back(d, i, nd)]
        remote(theirs, theirs, sds.at[i], sdr.at[i], {"dp": ring(d, i, nd)}).wait_recv()

    lead = layout.lead(c * nz + z)

    def finish(r, carry):
        at = pl.ds(pl.multiple_of(r * step_rows, step_rows), step_rows)
        total = d_buf[:, at, :].astype(jnp.float32)
        index = (
            lax.broadcasted_iota(jnp.int32, total.shape, 0) * rows
            + lax.broadcasted_iota(jnp.int32, total.shape, 1)
            + r * step_rows
        )
        total = jnp.where((index >= lead) & (index < lead + layout.used), total, 0.0)
        out_ref[:, at, :] = total
        return carry + jnp.sum((total * total).reshape(-1, 8, LANES), axis=0)

    sq_ref[0] = lax.fori_loop(
        0, rows // step_rows, finish, jnp.zeros((8, LANES), jnp.float32)
    )
    last = []
    for j in range(nc):
        for k in range(nz):
            slot = j * nz + k
            if slot:
                last.append(
                    start(
                        sq_ref.at[0],
                        sq_ref.at[slot],
                        sqs.at[slot],
                        sqr.at[slot],
                        {"ctx": ring(c, j, nc), "zero": ring(z, k, nz)},
                    )
                )
    for copy in last:
        copy.wait_recv()
    for copy in sends:
        copy.wait_send()


def reduce_grads(g, layout, nd, nc, nz):
    dma = pltpu.SemaphoreType.DMA
    rows = layout.part
    vmem = pl.BlockSpec(memory_space=pltpu.VMEM)
    return pl.pallas_call(
        functools.partial(reduce_kernel, nd, nc, nz, layout),
        out_shape=(
            jax.ShapeDtypeStruct((nd, rows, LANES), jnp.float32),
            jax.ShapeDtypeStruct((nc * nz, 8, LANES), jnp.float32),
        ),
        in_specs=[vmem],
        out_specs=(vmem, vmem),
        scratch_shapes=[
            pltpu.VMEM((nz, max(nc - 1, 1), layout.padded, LANES), jnp.bfloat16),
            pltpu.VMEM((nz, layout.padded, LANES), jnp.bfloat16),
            pltpu.VMEM((nz, max(nd - 1, 1), rows, LANES), jnp.bfloat16),
            pltpu.VMEM((nz, rows, LANES), jnp.bfloat16),
            pltpu.VMEM((nz, rows, LANES), jnp.bfloat16),
            pltpu.VMEM((nd, rows, LANES), jnp.bfloat16),
            dma((nz, nc)),
            dma((nz, nc)),
            dma((nz, nd)),
            dma((nz, nd)),
            dma((nz,)),
            dma((nz,)),
            dma((nd,)),
            dma((nd,)),
            dma((nc * nz,)),
            dma((nc * nz,)),
        ],
        compiler_params=pltpu.CompilerParams(
            collective_id=1, has_side_effects=True, vmem_limit_bytes=VMEM_LIMIT
        ),
        name="reduce_grads",
    )(g)


def share_kernel(nc, x_ref, out_ref, buf, own_sem, ssem, rsem):
    c = lax.axis_index("ctx")
    greet([{"ctx": ring(c, j, nc)} for j in range(1, nc)])
    copies = []
    for j in range(1, nc):
        copy = remote(x_ref, buf.at[j - 1], ssem.at[j], rsem.at[j], {"ctx": ring(c, j, nc)})
        copy.start()
        copies.append(copy)
    out_ref[c] = x_ref[...]
    for j in range(1, nc):
        copies[j - 1].wait()
        out_ref[back(c, j, nc)] = buf[j - 1]


def share_rows(x, nc):
    dma = pltpu.SemaphoreType.DMA
    vmem = pl.BlockSpec(memory_space=pltpu.VMEM)
    return pl.pallas_call(
        functools.partial(share_kernel, nc),
        out_shape=jax.ShapeDtypeStruct((nc,) + x.shape, x.dtype),
        in_specs=[vmem],
        out_specs=vmem,
        scratch_shapes=[
            pltpu.VMEM((max(nc - 1, 1),) + x.shape, x.dtype),
            dma,
            dma((nc,)),
            dma((nc,)),
        ],
        compiler_params=pltpu.CompilerParams(collective_id=2, has_side_effects=True),
        name="share_rows",
    )(x)


def sum_kernel(nc, x_ref, out_ref, buf, ssem, rsem):
    c = lax.axis_index("ctx")
    greet([{"ctx": ring(c, j, nc)} for j in range(1, nc)])
    copies = []
    for j in range(1, nc):
        copy = remote(
            x_ref.at[ring(c, j, nc)],
            buf.at[j - 1],
            ssem.at[j],
            rsem.at[j],
            {"ctx": ring(c, j, nc)},
        )
        copy.start()
        copies.append(copy)
    total = x_ref[c]
    for j in range(1, nc):
        copies[j - 1].wait()
        total = total + buf[j - 1]
    out_ref[...] = total


def sum_rows(x, nc):
    dma = pltpu.SemaphoreType.DMA
    vmem = pl.BlockSpec(memory_space=pltpu.VMEM)
    return pl.pallas_call(
        functools.partial(sum_kernel, nc),
        out_shape=jax.ShapeDtypeStruct(x.shape[1:], x.dtype),
        in_specs=[vmem],
        out_specs=vmem,
        scratch_shapes=[
            pltpu.VMEM((max(nc - 1, 1),) + x.shape[1:], x.dtype),
            dma((nc,)),
            dma((nc,)),
        ],
        compiler_params=pltpu.CompilerParams(collective_id=3, has_side_effects=True),
        name="sum_rows",
    )(x)


ALIGN = 16


class ShardRows:
    def __init__(self, shard_size, shards, parts):
        self.size = shard_size
        self.shards = shards
        self.whole = shard_size % LANES == 0
        self.used = -(-shard_size // LANES)
        spare = ALIGN - 1 if self.whole else 0
        self.part = -(-(self.used + spare) // (parts * 32)) * 32
        self.padded = parts * self.part
        self.total = self.base(shards - 1) + self.padded

    def base(self, index):
        if self.whole:
            return index * self.used // ALIGN * ALIGN
        return index * self.padded

    def lead(self, index):
        return index * self.used % ALIGN if self.whole else index * 0

    def place(self, flat, index):
        if not self.whole:
            extra = self.padded * LANES - self.size
            return jnp.pad(flat, (0, extra)).reshape(self.padded, LANES).astype(jnp.bfloat16)
        held = jnp.zeros((self.padded, LANES), flat.dtype)
        held = lax.dynamic_update_slice(
            held, flat.reshape(self.used, LANES), (self.lead(index), 0)
        )
        return held.astype(jnp.bfloat16)

    def pick(self, held, index):
        if not self.whole:
            return held.reshape(-1)[: self.size]
        return lax.dynamic_slice(held, (self.lead(index), 0), (self.used, LANES)).reshape(-1)

    def rows_of(self, full, low, high):
        pieces = []
        for index in range(self.shards):
            base = self.base(index)
            begin = base + (ALIGN if self.lead(index) else 0)
            end = index * self.used + self.used
            end = end // ALIGN * ALIGN if index + 1 < self.shards else end
            first, last = max(begin, low), min(end, high)
            if first < last:
                pieces.append(full[index, first - base : last - base])
            if index + 1 < self.shards and self.lead(index + 1) and low <= end < high:
                pieces.append(full[index, end - base : end - base + ALIGN] + full[index + 1, :ALIGN])
        return pieces[0] if len(pieces) == 1 else jnp.concatenate(pieces, axis=0)

    def unpack(self, full, model_width, head_count, head_dim, hidden):
        if not self.whole:
            flat = full.reshape(self.shards, -1)[:, : self.size].reshape(-1)
            return unpack(flat, model_width, head_count, head_dim, hidden)
        layouts = [
            (model_width, head_count * head_dim),
            (model_width, head_dim),
            (model_width, head_dim),
            (head_count * head_dim, model_width),
            (model_width, hidden),
            (model_width, hidden),
            (hidden, model_width),
        ]
        low = 0
        taken = []
        for layout in layouts:
            amount = layout[0] * layout[1] // LANES
            taken.append(self.rows_of(full, low, low + amount))
            low += amount
        taken.append(self.rows_of(full, low, self.shards * self.used))
        taken = lax.optimization_barrier(tuple(taken))
        pieces = [rows.reshape(layout) for rows, layout in zip(taken, layouts)]
        gains = taken[-1].reshape(-1)
        split = 4 * model_width
        pieces.append(gains[:split].reshape(4, model_width))
        pieces.append(gains[split:].reshape(2, head_dim))
        return pieces

    def pack(self, grads):
        if not self.whole:
            flat = jnp.concatenate([grad.reshape(-1) for grad in grads]).astype(jnp.bfloat16)
            flat = jnp.pad(
                flat.reshape(self.shards, -1), ((0, 0), (0, self.padded * LANES - self.size))
            )
            return flat.reshape(self.total, LANES)
        big = [grad.astype(jnp.bfloat16).reshape(-1, LANES) for grad in grads[:-2]]
        small = jnp.concatenate([grad.reshape(-1) for grad in grads[-2:]])
        rows = big + [small.astype(jnp.bfloat16).reshape(-1, LANES)]
        spare = self.total - sum(part.shape[0] for part in rows)
        return jnp.concatenate(rows + [jnp.zeros((spare, LANES), jnp.bfloat16)], axis=0)


def local(sizes, inputs, cotangent, params, first_moment, second_moment):
    tokens = inputs.shape[1]
    nd, nc, nz = sizes
    owner = lax.axis_index("ctx") * nz + lax.axis_index("zero")
    layout = ShardRows(params.shape[0], nc * nz, nd)
    own_b = layout.place(params, owner).reshape(nd, layout.part, LANES)
    gathered = gather_weights(own_b, nd, nc, nz).reshape(nc * nz, layout.padded, LANES)
    w_query, w_key, w_value, w_out, w_gate, w_up, w_down, norm_gains, head_gains = layout.unpack(
        gathered, D, HQ, HD, FF
    )
    norm_gains = norm_gains.astype(jnp.float32)
    head_gains = head_gains.astype(jnp.float32)
    positions = lax.axis_index("ctx") * tokens + jnp.arange(tokens, dtype=jnp.int32)
    cos_tab, sin_tab = rotary_tables(positions, HD)
    input_rows = inputs[0].astype(jnp.float32)
    normed_in, in_scale = rms_forward(input_rows, norm_gains[0])
    normed_b = normed_in.astype(jnp.bfloat16)
    queries = jnp.dot(normed_b, w_query, preferred_element_type=jnp.float32).reshape(tokens, HQ, HD)
    key_pre = jnp.dot(normed_b, w_key, preferred_element_type=jnp.float32)
    values = jnp.dot(normed_b, w_value, preferred_element_type=jnp.float32)
    q_normed, q_scale = rms_forward(queries, head_gains[0])
    k_normed, k_scale = rms_forward(key_pre, head_gains[1])
    query_scale = HD ** (-0.5)
    q_rot = (rotate(q_normed, cos_tab[:, None, :], sin_tab[:, None, :]) * query_scale).astype(
        jnp.bfloat16
    )
    k_rot = rotate(k_normed, cos_tab, sin_tab).astype(jnp.bfloat16)
    v_rows = values.astype(jnp.bfloat16)
    shared = share_rows(jnp.concatenate([k_rot, v_rows], axis=1), nc).reshape(nc * tokens, 2 * HD)
    all_keys, all_values = shared[:, :HD], shared[:, HD:]
    length = all_keys.shape[0]
    key_pos = jnp.arange(length, dtype=jnp.int32)
    block_rows = math.gcd(tokens, 512)
    blocks = tokens // block_rows
    q_blocks = q_rot.reshape(blocks, block_rows, HQ, HD)
    pos_blocks = positions.reshape(blocks, block_rows)

    def score_block(query_blk, pos_blk):
        scores = jnp.einsum("thd,sd->hts", query_blk, all_keys, preferred_element_type=jnp.float32)
        causal = key_pos[None, None, :] <= pos_blk[None, :, None]
        return (scores, causal)

    def forward_block(operands):
        query_blk, pos_blk = operands
        scores, causal = score_block(query_blk, pos_blk)
        row_total = jnp.sum(jnp.where(causal, jnp.exp(scores), 0.0), axis=-1)
        log_total = jnp.log(row_total)
        attn_probs = jnp.where(causal, jnp.exp(scores - log_total[..., None]), 0.0).astype(
            jnp.bfloat16
        )
        attended = jnp.einsum(
            "hts,sd->thd", attn_probs, all_values, preferred_element_type=jnp.float32
        )
        return (attended, log_total)

    attended, log_totals = lax.map(forward_block, (q_blocks, pos_blocks))
    attn_b = attended.reshape(tokens, HQ * HD).astype(jnp.bfloat16)
    attn_proj = jnp.dot(attn_b, w_out, preferred_element_type=jnp.float32)
    attn_normed, attn_scale = rms_forward(attn_proj, norm_gains[1])
    hidden_one = input_rows + attn_normed
    ffn_in, ffn_scale = rms_forward(hidden_one, norm_gains[2])
    ffn_b = ffn_in.astype(jnp.bfloat16)
    gate_pre = jnp.dot(ffn_b, w_gate, preferred_element_type=jnp.float32)
    up_proj = jnp.dot(ffn_b, w_up, preferred_element_type=jnp.float32)
    activated = gelu_value(gate_pre)
    mixed_b = (activated * up_proj).astype(jnp.bfloat16)
    ffn_proj = jnp.dot(mixed_b, w_down, preferred_element_type=jnp.float32)
    ffn_normed, out_scale = rms_forward(ffn_proj, norm_gains[3])
    out_rows = (hidden_one + ffn_normed).astype(jnp.bfloat16)
    grad_rows = cotangent[0].astype(jnp.float32)
    d_ffn_proj, g_gain_three = rms_backward(ffn_proj, out_scale, norm_gains[3], grad_rows)
    d_ffn_b = d_ffn_proj.astype(jnp.bfloat16)
    grad_down = jnp.dot(mixed_b.T, d_ffn_b, preferred_element_type=jnp.float32)
    d_mixed = jnp.dot(d_ffn_b, w_down.T, preferred_element_type=jnp.float32)
    d_gate_b = (d_mixed * up_proj * gelu_slope(gate_pre)).astype(jnp.bfloat16)
    d_up_b = (d_mixed * activated).astype(jnp.bfloat16)
    grad_gate = jnp.dot(ffn_b.T, d_gate_b, preferred_element_type=jnp.float32)
    grad_up = jnp.dot(ffn_b.T, d_up_b, preferred_element_type=jnp.float32)
    d_ffn_in = jnp.dot(d_gate_b, w_gate.T, preferred_element_type=jnp.float32) + jnp.dot(
        d_up_b, w_up.T, preferred_element_type=jnp.float32
    )
    d_hidden_part, g_gain_two = rms_backward(hidden_one, ffn_scale, norm_gains[2], d_ffn_in)
    d_hidden_one = grad_rows + d_hidden_part
    d_attn_proj, g_gain_one = rms_backward(attn_proj, attn_scale, norm_gains[1], d_hidden_one)
    d_attn_b = d_attn_proj.astype(jnp.bfloat16)
    grad_out = jnp.dot(attn_b.T, d_attn_b, preferred_element_type=jnp.float32)
    d_heads = (
        jnp.dot(d_attn_b, w_out.T, preferred_element_type=jnp.float32)
        .astype(jnp.bfloat16)
        .reshape(tokens, HQ, HD)
    )
    attn_heads = attn_b.reshape(tokens, HQ, HD)
    row_delta = jnp.sum(d_heads.astype(jnp.float32) * attn_heads.astype(jnp.float32), axis=-1)
    delta_blocks = row_delta.reshape(blocks, block_rows, HQ)
    dout_blocks = d_heads.reshape(blocks, block_rows, HQ, HD)

    def backward_block(running, operands):
        key_acc, value_acc = running
        query_blk, pos_blk, lse_blk, dout_blk, delta_blk = operands
        scores, causal = score_block(query_blk, pos_blk)
        attn_probs = jnp.where(causal, jnp.exp(scores - lse_blk[..., None]), 0.0).astype(
            jnp.bfloat16
        )
        d_probs = jnp.einsum(
            "thd,sd->hts", dout_blk, all_values, preferred_element_type=jnp.float32
        )
        d_scores = (
            attn_probs.astype(jnp.float32) * (d_probs - jnp.transpose(delta_blk)[:, :, None])
        ).astype(jnp.bfloat16)
        value_acc = value_acc + jnp.einsum(
            "hts,thd->sd", attn_probs, dout_blk, preferred_element_type=jnp.float32
        )
        key_acc = key_acc + jnp.einsum(
            "hts,thd->sd", d_scores, query_blk, preferred_element_type=jnp.float32
        )
        d_query = jnp.einsum("hts,sd->thd", d_scores, all_keys, preferred_element_type=jnp.float32)
        return ((key_acc, value_acc), d_query)

    zero_rows = jnp.zeros((length, HD), jnp.float32)
    (key_terms, value_terms), d_queries = lax.scan(
        backward_block,
        (zero_rows, zero_rows),
        (q_blocks, pos_blocks, log_totals, dout_blocks, delta_blocks),
    )
    d_both = sum_rows(
        jnp.concatenate([key_terms, value_terms], axis=1).reshape(nc, tokens, 2 * HD), nc
    )
    d_keys, d_values = d_both[:, :HD], d_both[:, HD:]
    d_queries = d_queries.reshape(tokens, HQ, HD)
    d_q_normed = rotate_back(d_queries * query_scale, cos_tab[:, None, :], sin_tab[:, None, :])
    d_k_normed = rotate_back(d_keys, cos_tab, sin_tab)
    d_query_pre, g_head_query = rms_backward(queries, q_scale, head_gains[0], d_q_normed)
    d_key_pre, g_head_key = rms_backward(key_pre, k_scale, head_gains[1], d_k_normed)
    dq_b = d_query_pre.reshape(tokens, HQ * HD).astype(jnp.bfloat16)
    dk_b = d_key_pre.astype(jnp.bfloat16)
    dv_b = d_values.astype(jnp.bfloat16)
    grad_query = jnp.dot(normed_b.T, dq_b, preferred_element_type=jnp.float32)
    grad_key = jnp.dot(normed_b.T, dk_b, preferred_element_type=jnp.float32)
    grad_value = jnp.dot(normed_b.T, dv_b, preferred_element_type=jnp.float32)
    d_normed = (
        jnp.dot(dq_b, w_query.T, preferred_element_type=jnp.float32)
        + jnp.dot(dk_b, w_key.T, preferred_element_type=jnp.float32)
        + jnp.dot(dv_b, w_value.T, preferred_element_type=jnp.float32)
    )
    d_input_part, g_gain_zero = rms_backward(input_rows, in_scale, norm_gains[0], d_normed)
    d_input = (d_hidden_one + d_input_part)[None]
    packed = layout.pack(
        [
            grad_query,
            grad_key,
            grad_value,
            grad_out,
            grad_gate,
            grad_up,
            grad_down,
            jnp.stack([g_gain_zero, g_gain_one, g_gain_two, g_gain_three]),
            jnp.stack([g_head_query, g_head_key]),
        ]
    )
    total_params = layout.shards * layout.size
    summed, square_parts = reduce_grads(packed, layout, nd, nc, nz)
    summed = layout.pick(summed.reshape(layout.padded, LANES), owner)
    squares = jnp.sum(square_parts)
    new_params, new_first, new_second = adam_update(
        params, first_moment, second_moment, summed, clip_factor(squares, total_params)
    )
    return (out_rows[None], d_input, new_params, new_first, new_second, summed)


def solution(mesh):
    sizes = tuple(mesh.shape[axis] for axis in ("dp", "ctx", "zero"))
    placed = (
        P(("dp", "zero"), "ctx", None),
        P(("dp", "zero"), "ctx", None),
        P(("ctx", "zero")),
        P(("ctx", "zero")),
        P(("ctx", "zero")),
    )
    return jax.shard_map(
        functools.partial(local, sizes),
        mesh=mesh,
        in_specs=placed,
        out_specs=(
            P(("dp", "zero"), "ctx", None),
            P(("dp", "zero"), "ctx", None),
            P(("ctx", "zero")),
            P(("ctx", "zero")),
            P(("ctx", "zero")),
            P(("ctx", "zero")),
        ),
        check_vma=False,
    )
```

```python
import functools
import math

import jax
import jax.numpy as jnp
from jax import lax
from jax.experimental import pallas as pl
from jax.experimental.pallas import tpu as pltpu
from jax.sharding import PartitionSpec as P

D = 640
HQ = 4
HD = 256
FF = 2048


norm_eps = 1e-06
rope_base = 1000000.0
beta_one = 0.9
beta_two = 0.999
learn_rate = 0.01
decay_rate = 0.1
adam_eps = 1e-08
adam_step = 3
gelu_coef = 0.7978845608028654


def gelu_value(pre_act):
    tanh_part = jnp.tanh(gelu_coef * (pre_act + 0.044715 * pre_act * pre_act * pre_act))
    return 0.5 * pre_act * (1.0 + tanh_part)


def gelu_slope(pre_act):
    tanh_part = jnp.tanh(gelu_coef * (pre_act + 0.044715 * pre_act * pre_act * pre_act))
    return 0.5 * (1.0 + tanh_part) + 0.5 * pre_act * (1.0 - tanh_part * tanh_part) * gelu_coef * (
        1.0 + 3.0 * 0.044715 * pre_act * pre_act
    )


def rms_forward(values_in, gain_row):
    inv_rms = lax.rsqrt(jnp.mean(values_in * values_in, axis=-1, keepdims=True) + norm_eps)
    return (values_in * inv_rms * (1.0 + gain_row), inv_rms)


def rms_backward(values_in, inv_rms, gain_row, grad_out):
    weighted = grad_out * (1.0 + gain_row)
    grad_in = inv_rms * (
        weighted
        - values_in * inv_rms * inv_rms * jnp.mean(weighted * values_in, axis=-1, keepdims=True)
    )
    leading = tuple(range(values_in.ndim - 1))
    grad_gain = jnp.sum(grad_out * values_in * inv_rms, axis=leading)
    return (grad_in, grad_gain)


def rotary_tables(positions, head_dim):
    half_dim = head_dim // 2
    freqs = jnp.exp(
        jnp.arange(half_dim, dtype=jnp.float32) * (-2.0 * math.log(rope_base) / head_dim)
    )
    angles = positions.astype(jnp.float32)[:, None] * freqs[None, :]
    return (jnp.cos(angles), jnp.sin(angles))


def rotate(tensor, cos_part, sin_part):
    half_dim = tensor.shape[-1] // 2
    first_half = tensor[..., :half_dim]
    second_half = tensor[..., half_dim:]
    return jnp.concatenate(
        [
            first_half * cos_part - second_half * sin_part,
            second_half * cos_part + first_half * sin_part,
        ],
        axis=-1,
    )


def rotate_back(tensor, cos_part, sin_part):
    half_dim = tensor.shape[-1] // 2
    first_half = tensor[..., :half_dim]
    second_half = tensor[..., half_dim:]
    return jnp.concatenate(
        [
            first_half * cos_part + second_half * sin_part,
            second_half * cos_part - first_half * sin_part,
        ],
        axis=-1,
    )


def weight_layouts(model_width, head_count, head_dim, hidden):
    return [
        (model_width, head_count * head_dim),
        (model_width, head_dim),
        (model_width, head_dim),
        (head_count * head_dim, model_width),
        (model_width, hidden),
        (model_width, hidden),
        (hidden, model_width),
        (4, model_width),
        (2, head_dim),
    ]


def unpack(flat_values, model_width, head_count, head_dim, hidden):
    layouts = weight_layouts(model_width, head_count, head_dim, hidden)
    pieces = []
    offset = 0
    for layout in layouts:
        amount = layout[0] * layout[1]
        pieces.append(flat_values[offset : offset + amount].reshape(layout))
        offset += amount
    return pieces


def adam_update(weights, moment_one, moment_two, grad_values, clip_scale):
    clipped = grad_values * clip_scale
    new_one = beta_one * moment_one + (1.0 - beta_one) * clipped
    new_two = beta_two * moment_two + (1.0 - beta_two) * clipped * clipped
    corrected_one = new_one / (1.0 - beta_one**adam_step)
    corrected_two = new_two / (1.0 - beta_two**adam_step)
    new_weights = weights - learn_rate * (
        corrected_one / (jnp.sqrt(corrected_two) + adam_eps) + decay_rate * weights
    )
    return (new_weights, new_one, new_two)


def clip_factor(squares, amount):
    return jnp.minimum(1.0, lax.rsqrt(squares / amount + 1e-06))


MESH_ID = pl.DeviceIdType.MESH
LANES = 128
VMEM_LIMIT = 60 * 1024 * 1024


def ring(position, step, size):
    return lax.rem(position + step, size)


def back(position, step, size):
    return lax.rem(position + size - step, size)


def greet(peers):
    barrier = pltpu.get_barrier_semaphore()
    for peer in peers:
        pl.semaphore_signal(barrier, inc=1, device_id=peer, device_id_type=MESH_ID)
    pl.semaphore_wait(barrier, len(peers))


def remote(src, dst, send_sem, recv_sem, peer):
    return pltpu.make_async_remote_copy(
        src_ref=src,
        dst_ref=dst,
        send_sem=send_sem,
        recv_sem=recv_sem,
        device_id=peer,
        device_id_type=MESH_ID,
    )


def quarter(ref, part, rows, first=0, amount=None):
    amount = rows if amount is None else amount
    return ref.at[pl.ds(pl.multiple_of(part * rows + first, ALIGN), amount)]


def square(d):
    return d + 1 - 2 * lax.rem(d, 2), lax.rem(d + 2, 4)


def gather_kernel(nd, nc, nz, layout, plan, x_ref, *refs):
    outs = refs[: len(plan)]
    full_ref, own_sem, s1s, s1r, s2s, s2r, s3s, s3r, sos, sor, out_sem = refs[len(plan) :]
    d = lax.axis_index("dp")
    c = lax.axis_index("ctx")
    z = lax.axis_index("zero")
    rows = layout.part
    half = rows // 2
    greet(
        [{"zero": ring(z, k, nz)} for k in range(1, nz)]
        + [{"dp": ring(d, i, nd)} for i in range(1, nd)]
        + [{"ctx": ring(c, j, nc)} for j in range(1, nc)]
    )
    sends = []

    def start(src, dst, ssem, rsem, peer):
        copy = remote(src, dst, ssem, rsem, peer)
        copy.start()
        sends.append(copy)

    def piece_of(col, row, part, first=0, amount=None):
        return quarter(full_ref.at[col, row], part, rows, first, amount)

    def arrived(ref, sem, peer):
        remote(ref, ref, s1s.at[0], sem, peer).wait_recv()

    for k in range(1, nz):
        start(
            quarter(x_ref, d, rows), piece_of(c, z, d), s1s.at[k], s1r.at[k],
            {"zero": ring(z, k, nz)},
        )
    own = pltpu.make_async_copy(x_ref, full_ref.at[c, z], own_sem)
    own.start()
    for j in range(1, nc):
        start(x_ref, full_ref.at[c, z], sos.at[j], sor.at[j], {"ctx": ring(c, j, nc)})

    def to_ctx(piece, k, i):
        for j in range(1, nc):
            start(piece, piece, s3s.at[k, i, j], s3r.at[k, i, j], {"ctx": ring(c, j, nc)})

    paired = nd == 4
    if paired:
        near_x, near_y = square(d)
        far = 3 - d
        hops = [(1, near_x), (2, near_y)]
    else:
        hops = [(i, ring(d, i, nd)) for i in range(1, nd)]
    for k in range(1, nz):
        piece = piece_of(c, back(z, k, nz), d)
        arrived(piece, s1r.at[k], {"zero": ring(z, k, nz)})
        for i, peer in hops:
            start(piece, piece, s2s.at[k, i], s2r.at[k, i], {"dp": peer})
        to_ctx(piece, k, 0)
    for k in range(1, nz):
        src_z = back(z, k, nz)
        for i, peer in hops:
            origin = peer if paired else back(d, i, nd)
            piece = piece_of(c, src_z, origin)
            arrived(piece, s2r.at[k, i], {"dp": peer})
            if paired:
                onward = piece_of(c, src_z, origin, (i - 1) * half, half)
                other = near_y if i == 1 else near_x
                start(onward, onward, s2s.at[k, 2 + i], s2r.at[k, 2 + i], {"dp": other})
            to_ctx(piece, k, i)
    if paired:
        for k in range(1, nz):
            src_z = back(z, k, nz)
            for i, peer in ((1, near_y), (2, near_x)):
                piece = piece_of(c, src_z, far, (i - 1) * half, half)
                arrived(piece, s2r.at[k, 2 + i], {"dp": peer})
            to_ctx(piece_of(c, src_z, far), k, 3)
    for j in range(1, nc):
        src_c = back(c, j, nc)
        peer = {"ctx": ring(c, j, nc)}
        arrived(full_ref.at[src_c, z], sor.at[j], peer)
        for k in range(1, nz):
            src_z = back(z, k, nz)
            if paired:
                origins = (d, near_x, near_y, far)
            else:
                origins = [back(d, i, nd) for i in range(nd)]
            for i, origin in enumerate(origins):
                arrived(piece_of(src_c, src_z, origin), s3r.at[k, i, j], peer)
    for copy in sends:
        copy.wait_send()
    own.wait()
    for index in range(layout.shards - 1):
        if layout.lead(index + 1):
            tail = pl.ds(layout.base(index + 1) - layout.base(index), ALIGN)
            here = divmod(index, nz)
            there = divmod(index + 1, nz)
            full_ref[here[0], here[1], tail, :] = (
                full_ref[here[0], here[1], tail, :] + full_ref[there[0], there[1], pl.ds(0, ALIGN), :]
            )
    moves = []
    for out, segments in zip(outs, plan):
        for index, src, dst, amount in segments:
            move = pltpu.make_async_copy(
                full_ref.at[index // nz, index % nz, pl.ds(src, amount)],
                out.at[pl.ds(dst, amount)],
                out_sem.at[len(moves)],
            )
            move.start()
            moves.append(move)
    for move in moves:
        move.wait()


def gather_weights(x, layout, plan, nd, nc, nz):
    dma = pltpu.SemaphoreType.DMA
    anywhere = pl.BlockSpec(memory_space=pl.ANY)
    return pl.pallas_call(
        functools.partial(gather_kernel, nd, nc, nz, layout, plan),
        out_shape=[
            jax.ShapeDtypeStruct((sum(part[3] for part in segments), LANES), x.dtype)
            for segments in plan
        ],
        in_specs=[pl.BlockSpec(memory_space=pltpu.VMEM)],
        out_specs=[anywhere] * len(plan),
        scratch_shapes=[
            pltpu.VMEM((nc, nz, layout.padded, LANES), x.dtype),
            dma,
            dma((nz,)),
            dma((nz,)),
            dma((nz, nd + 1)),
            dma((nz, nd + 1)),
            dma((nz, nd, nc)),
            dma((nz, nd, nc)),
            dma((nc,)),
            dma((nc,)),
            dma((sum(len(segments) for segments in plan),)),
        ],
        compiler_params=pltpu.CompilerParams(
            collective_id=0, has_side_effects=True, vmem_limit_bytes=VMEM_LIMIT
        ),
        name="gather_weights",
    )(x)


def reduce_kernel(
    nd, nc, nz, layout, offsets, *refs
):
    g_parts = refs[: len(offsets)]
    (
        out_ref, sq_ref, g_ref, a_buf, b_src, b_buf, b_mid, b_two, c_src, c_buf, d_buf,
        g_sem, sas, sar, sbs, sbr, scs, scr, sds, sdr, sqs, sqr,
    ) = refs[len(offsets) :]
    loads = []
    for index, offset in enumerate(offsets):
        load = pltpu.make_async_copy(
            g_parts[index],
            g_ref.at[pl.ds(offset, g_parts[index].shape[0])],
            g_sem.at[index],
        )
        load.start()
        loads.append(load)
    d = lax.axis_index("dp")
    c = lax.axis_index("ctx")
    z = lax.axis_index("zero")
    step_rows = 32
    rows = layout.part

    def base(col, row):
        return pl.multiple_of(layout.base(col * nz + row), ALIGN)

    greet(
        [
            {"ctx": ring(c, j, nc), "zero": ring(z, k, nz)}
            for j in range(nc)
            for k in range(nz)
            if j or k
        ]
        + [{"dp": ring(d, i, nd)} for i in range(1, nd)]
    )
    sends = []

    def start(src, dst, ssem, rsem, peer):
        copy = remote(src, dst, ssem, rsem, peer)
        copy.start()
        sends.append(copy)
        return copy

    for load in loads:
        load.wait()
    paired = nd == 4
    half = rows // 2
    if paired:
        near_x, near_y = square(d)
        far = 3 - d
    first = []
    for k in range(nz):
        dst_z = ring(z, k + 1, nz)
        first.append(
            [
                start(
                    g_ref.at[pl.ds(base(ring(c, j, nc), dst_z), layout.padded)],
                    a_buf.at[k, j - 1],
                    sas.at[k, j],
                    sar.at[k, j],
                    {"ctx": ring(c, j, nc)},
                )
                for j in range(1, nc)
            ]
        )
    second = []
    for k in range(nz):
        dst_z = ring(z, k + 1, nz)
        for copy in first[k]:
            copy.wait_recv()

        def add_ctx(r, carry, k=k, dst_z=dst_z):
            at = pl.ds(pl.multiple_of(r * step_rows, step_rows), step_rows)
            mine = pl.ds(pl.multiple_of(base(c, dst_z) + r * step_rows, ALIGN), step_rows)
            total = g_ref[mine, :].astype(jnp.float32)
            for j in range(1, nc):
                total = total + a_buf[k, j - 1, at, :].astype(jnp.float32)
            b_src[k, at, :] = total.astype(jnp.bfloat16)
            return carry

        lax.fori_loop(0, layout.padded // step_rows, add_ctx, 0, unroll=4)
        if paired:
            second.append(
                [
                    start(
                        quarter(b_src.at[k], part, rows, lot * half, half),
                        b_buf.at[k, 2 * lot + place],
                        sbs.at[k, 2 * lot + place],
                        sbr.at[k, 2 * lot + place],
                        {"dp": peer},
                    )
                    for lot, place, part, peer in (
                        (0, 1, far, near_x),
                        (1, 1, far, near_y),
                        (0, 0, near_x, near_x),
                        (1, 0, near_y, near_y),
                    )
                ]
            )
            continue
        second.append(
            [
                start(
                    b_src.at[k, pl.ds(pl.multiple_of(ring(d, i, nd) * rows, 32), rows)],
                    b_buf.at[k, i - 1],
                    sbs.at[k, i],
                    sbr.at[k, i],
                    {"dp": ring(d, i, nd)},
                )
                for i in range(1, nd)
            ]
        )
    middle = []
    for k in range(nz if paired else 0):
        for copy in second[k]:
            copy.wait_recv()

        def add_near(r, carry, k=k):
            at = pl.ds(pl.multiple_of(r * ALIGN, ALIGN), ALIGN)
            for lot, part in ((0, near_y), (1, near_x)):
                mine = pl.ds(
                    pl.multiple_of(part * rows + lot * half + r * ALIGN, ALIGN), ALIGN
                )
                total = b_src[k, mine, :].astype(jnp.float32)
                total = total + b_buf[k, 2 * lot + 1, at, :].astype(jnp.float32)
                b_mid[k, lot, at, :] = total.astype(jnp.bfloat16)
            return carry

        lax.fori_loop(0, half // ALIGN, add_near, 0)
        middle.append(
            [
                start(
                    b_mid.at[k, lot],
                    b_two.at[k, lot],
                    sbs.at[k, 4 + lot],
                    sbr.at[k, 4 + lot],
                    {"dp": peer},
                )
                for lot, peer in ((0, near_y), (1, near_x))
            ]
        )
    third = []
    for k in range(nz):
        for copy in middle[k] if paired else second[k]:
            copy.wait_recv()

        def add_dp(r, carry, k=k):
            at = pl.ds(pl.multiple_of(r * step_rows, step_rows), step_rows)
            mine = pl.ds(pl.multiple_of(d * rows + r * step_rows, step_rows), step_rows)
            total = b_src[k, mine, :].astype(jnp.float32)
            for i in range(1, nd):
                total = total + b_buf[k, i - 1, at, :].astype(jnp.float32)
            c_src[k, at, :] = total.astype(jnp.bfloat16)
            return carry

        def add_pair(r, carry, k=k):
            at = pl.ds(pl.multiple_of(r * ALIGN, ALIGN), ALIGN)
            for lot in range(2):
                mine = pl.ds(pl.multiple_of(d * rows + lot * half + r * ALIGN, ALIGN), ALIGN)
                total = b_src[k, mine, :].astype(jnp.float32)
                total = total + b_buf[k, 2 * lot, at, :].astype(jnp.float32)
                total = total + b_two[k, lot, at, :].astype(jnp.float32)
                put = pl.ds(pl.multiple_of(lot * half + r * ALIGN, ALIGN), ALIGN)
                c_src[k, put, :] = total.astype(jnp.bfloat16)
            return carry

        if paired:
            lax.fori_loop(0, half // ALIGN, add_pair, 0)
        else:
            lax.fori_loop(0, rows // step_rows, add_dp, 0)
        if k < nz - 1:
            third.append(
                start(
                    c_src.at[k],
                    c_buf.at[k],
                    scs.at[k],
                    scr.at[k],
                    {"zero": ring(z, k + 1, nz)},
                )
            )
    for copy in third:
        copy.wait_recv()

    def add_zero(r, carry):
        at = pl.ds(pl.multiple_of(r * step_rows, step_rows), step_rows)
        total = c_src[nz - 1, at, :].astype(jnp.float32)
        for k in range(nz - 1):
            total = total + c_buf[k, at, :].astype(jnp.float32)
        d_buf[d, at, :] = total.astype(jnp.bfloat16)
        return carry

    lax.fori_loop(0, rows // step_rows, add_zero, 0)
    mine = d_buf.at[d]
    for i in range(1, nd):
        start(mine, mine, sds.at[i], sdr.at[i], {"dp": ring(d, i, nd)})
    for i in range(1, nd):
        theirs = d_buf.at[back(d, i, nd)]
        remote(theirs, theirs, sds.at[i], sdr.at[i], {"dp": ring(d, i, nd)}).wait_recv()

    lead = layout.lead(c * nz + z)

    def finish(r, carry):
        at = pl.ds(pl.multiple_of(r * step_rows, step_rows), step_rows)
        total = d_buf[:, at, :].astype(jnp.float32)
        index = (
            lax.broadcasted_iota(jnp.int32, total.shape, 0) * rows
            + lax.broadcasted_iota(jnp.int32, total.shape, 1)
            + r * step_rows
        )
        total = jnp.where((index >= lead) & (index < lead + layout.used), total, 0.0)
        out_ref[:, at, :] = total
        return carry + jnp.sum((total * total).reshape(-1, 8, LANES), axis=0)

    sq_ref[0] = lax.fori_loop(
        0, rows // step_rows, finish, jnp.zeros((8, LANES), jnp.float32)
    )
    last = []
    for j in range(nc):
        for k in range(nz):
            slot = j * nz + k
            if slot:
                last.append(
                    start(
                        sq_ref.at[0],
                        sq_ref.at[slot],
                        sqs.at[slot],
                        sqr.at[slot],
                        {"ctx": ring(c, j, nc), "zero": ring(z, k, nz)},
                    )
                )
    for copy in last:
        copy.wait_recv()
    for copy in sends:
        copy.wait_send()


def reduce_grads(parts, offsets, layout, nd, nc, nz):
    dma = pltpu.SemaphoreType.DMA
    rows = layout.part
    vmem = pl.BlockSpec(memory_space=pltpu.VMEM)
    return pl.pallas_call(
        functools.partial(reduce_kernel, nd, nc, nz, layout, offsets),
        out_shape=(
            jax.ShapeDtypeStruct((nd, rows, LANES), jnp.float32),
            jax.ShapeDtypeStruct((nc * nz, 8, LANES), jnp.float32),
        ),
        in_specs=[pl.BlockSpec(memory_space=pl.ANY)] * len(parts),
        out_specs=(vmem, vmem),
        scratch_shapes=[
            pltpu.VMEM((layout.total, LANES), jnp.bfloat16),
            pltpu.VMEM((nz, max(nc - 1, 1), layout.padded, LANES), jnp.bfloat16),
            pltpu.VMEM((nz, layout.padded, LANES), jnp.bfloat16),
            pltpu.VMEM(
                (nz, 4, rows // 2, LANES) if nd == 4 else (nz, max(nd - 1, 1), rows, LANES),
                jnp.bfloat16,
            ),
            pltpu.VMEM((nz, 2, rows // 2, LANES), jnp.bfloat16),
            pltpu.VMEM((nz, 2, rows // 2, LANES), jnp.bfloat16),
            pltpu.VMEM((nz, rows, LANES), jnp.bfloat16),
            pltpu.VMEM((nz, rows, LANES), jnp.bfloat16),
            pltpu.VMEM((nd, rows, LANES), jnp.bfloat16),
            dma((len(parts),)),
            dma((nz, nc)),
            dma((nz, nc)),
            dma((nz, nd + 2)),
            dma((nz, nd + 2)),
            dma((nz,)),
            dma((nz,)),
            dma((nd,)),
            dma((nd,)),
            dma((nc * nz,)),
            dma((nc * nz,)),
        ],
        compiler_params=pltpu.CompilerParams(
            collective_id=1, has_side_effects=True, vmem_limit_bytes=VMEM_LIMIT
        ),
        name="reduce_grads",
    )(*parts)


def share_kernel(nc, x_ref, out_ref, buf, own_sem, ssem, rsem):
    c = lax.axis_index("ctx")
    greet([{"ctx": ring(c, j, nc)} for j in range(1, nc)])
    copies = []
    for j in range(1, nc):
        copy = remote(x_ref, buf.at[j - 1], ssem.at[j], rsem.at[j], {"ctx": ring(c, j, nc)})
        copy.start()
        copies.append(copy)
    out_ref[c] = x_ref[...]
    for j in range(1, nc):
        copies[j - 1].wait()
        out_ref[back(c, j, nc)] = buf[j - 1]


def share_rows(x, nc):
    dma = pltpu.SemaphoreType.DMA
    vmem = pl.BlockSpec(memory_space=pltpu.VMEM)
    return pl.pallas_call(
        functools.partial(share_kernel, nc),
        out_shape=jax.ShapeDtypeStruct((nc,) + x.shape, x.dtype),
        in_specs=[vmem],
        out_specs=vmem,
        scratch_shapes=[
            pltpu.VMEM((max(nc - 1, 1),) + x.shape, x.dtype),
            dma,
            dma((nc,)),
            dma((nc,)),
        ],
        compiler_params=pltpu.CompilerParams(collective_id=2, has_side_effects=True),
        name="share_rows",
    )(x)


def sum_kernel(nc, x_ref, out_ref, buf, ssem, rsem):
    c = lax.axis_index("ctx")
    greet([{"ctx": ring(c, j, nc)} for j in range(1, nc)])
    copies = []
    for j in range(1, nc):
        copy = remote(
            x_ref.at[ring(c, j, nc)],
            buf.at[j - 1],
            ssem.at[j],
            rsem.at[j],
            {"ctx": ring(c, j, nc)},
        )
        copy.start()
        copies.append(copy)
    total = x_ref[c]
    for j in range(1, nc):
        copies[j - 1].wait()
        total = total + buf[j - 1]
    out_ref[...] = total


def sum_rows(x, nc):
    dma = pltpu.SemaphoreType.DMA
    vmem = pl.BlockSpec(memory_space=pltpu.VMEM)
    return pl.pallas_call(
        functools.partial(sum_kernel, nc),
        out_shape=jax.ShapeDtypeStruct(x.shape[1:], x.dtype),
        in_specs=[vmem],
        out_specs=vmem,
        scratch_shapes=[
            pltpu.VMEM((max(nc - 1, 1),) + x.shape[1:], x.dtype),
            dma((nc,)),
            dma((nc,)),
        ],
        compiler_params=pltpu.CompilerParams(collective_id=3, has_side_effects=True),
        name="sum_rows",
    )(x)


ALIGN = 16


class ShardRows:
    def __init__(self, shard_size, shards, parts):
        self.size = shard_size
        self.shards = shards
        self.whole = shard_size % LANES == 0
        self.used = -(-shard_size // LANES)
        spare = ALIGN - 1 if self.whole else 0
        self.part = -(-(self.used + spare) // (parts * 32)) * 32
        self.padded = parts * self.part
        self.total = self.base(shards - 1) + self.padded

    def base(self, index):
        if self.whole:
            return index * self.used // ALIGN * ALIGN
        return index * self.padded

    def lead(self, index):
        return index * self.used % ALIGN if self.whole else index * 0

    def place(self, flat, index):
        if not self.whole:
            extra = self.padded * LANES - self.size
            return jnp.pad(flat, (0, extra)).reshape(self.padded, LANES).astype(jnp.bfloat16)
        held = jnp.zeros((self.padded, LANES), flat.dtype)
        held = lax.dynamic_update_slice(
            held, flat.reshape(self.used, LANES), (self.lead(index), 0)
        )
        return held.astype(jnp.bfloat16)

    def pick(self, held, index):
        if not self.whole:
            return held.reshape(-1)[: self.size]
        return lax.dynamic_slice(held, (self.lead(index), 0), (self.used, LANES)).reshape(-1)

    def begin(self, index):
        return self.base(index) + (ALIGN if self.lead(index) else 0)

    def segments(self, low, high):
        found = []
        for index in range(self.shards):
            last = self.base(index) + self.padded
            if index + 1 < self.shards:
                last = self.begin(index + 1)
            first, last = max(self.begin(index), low), min(last, high)
            if first < last:
                found.append((index, first - self.base(index), first - low, last - first))
        return found

    def plan(self, layouts):
        if not self.whole:
            return [self.segments(0, self.total)]
        low = 0
        plans = []
        for layout in layouts[:-2]:
            amount = layout[0] * layout[1] // LANES
            plans.append(self.segments(low, low + amount))
            low += amount
        high = -(-self.shards * self.used // ALIGN) * ALIGN
        plans.append(self.segments(low, high))
        return plans

    def unpack(self, taken, layouts, sizes):
        if not self.whole:
            flat = taken[0].reshape(self.shards, -1)[:, : self.size].reshape(-1)
            return unpack(flat, *sizes)
        pieces = [rows.reshape(layout) for rows, layout in zip(taken, layouts[:-2])]
        gains = taken[-1].reshape(-1)
        low = 0
        for layout in layouts[-2:]:
            amount = layout[0] * layout[1]
            pieces.append(gains[low : low + amount].reshape(layout))
            low += amount
        return pieces

    def pack(self, grads):
        if not self.whole:
            flat = jnp.concatenate([grad.reshape(-1) for grad in grads]).astype(jnp.bfloat16)
            flat = jnp.pad(
                flat.reshape(self.shards, -1), ((0, 0), (0, self.padded * LANES - self.size))
            )
            return [flat.reshape(self.total, LANES)], [0]
        parts = [grad.astype(jnp.bfloat16).reshape(-1, LANES) for grad in grads[:-2]]
        offsets = [0]
        for part in parts:
            offsets.append(offsets[-1] + part.shape[0])
        small = jnp.concatenate([grad.reshape(-1) for grad in grads[-2:]])
        small = small.astype(jnp.bfloat16).reshape(-1, LANES)
        spare = self.total - offsets[-1] - small.shape[0]
        parts.append(jnp.pad(small, ((0, spare), (0, 0))))
        return parts, offsets


def local(sizes, inputs, cotangent, params, first_moment, second_moment):
    tokens = inputs.shape[1]
    nd, nc, nz = sizes
    owner = lax.axis_index("ctx") * nz + lax.axis_index("zero")
    layout = ShardRows(params.shape[0], nc * nz, nd)
    layouts = weight_layouts(D, HQ, HD, FF)
    own_b = layout.place(params, owner)
    gathered = gather_weights(own_b, layout, layout.plan(layouts), nd, nc, nz)
    w_query, w_key, w_value, w_out, w_gate, w_up, w_down, norm_gains, head_gains = layout.unpack(
        gathered, layouts, (D, HQ, HD, FF)
    )
    norm_gains = norm_gains.astype(jnp.float32)
    head_gains = head_gains.astype(jnp.float32)
    positions = lax.axis_index("ctx") * tokens + jnp.arange(tokens, dtype=jnp.int32)
    cos_tab, sin_tab = rotary_tables(positions, HD)
    input_rows = inputs[0].astype(jnp.float32)
    normed_in, in_scale = rms_forward(input_rows, norm_gains[0])
    normed_b = normed_in.astype(jnp.bfloat16)
    queries = jnp.dot(normed_b, w_query, preferred_element_type=jnp.float32).reshape(tokens, HQ, HD)
    key_pre = jnp.dot(normed_b, w_key, preferred_element_type=jnp.float32)
    values = jnp.dot(normed_b, w_value, preferred_element_type=jnp.float32)
    q_normed, q_scale = rms_forward(queries, head_gains[0])
    k_normed, k_scale = rms_forward(key_pre, head_gains[1])
    query_scale = HD ** (-0.5)
    q_rot = (rotate(q_normed, cos_tab[:, None, :], sin_tab[:, None, :]) * query_scale).astype(
        jnp.bfloat16
    )
    k_rot = rotate(k_normed, cos_tab, sin_tab).astype(jnp.bfloat16)
    v_rows = values.astype(jnp.bfloat16)
    shared = share_rows(jnp.concatenate([k_rot, v_rows], axis=1), nc).reshape(nc * tokens, 2 * HD)
    all_keys, all_values = shared[:, :HD], shared[:, HD:]
    length = all_keys.shape[0]
    key_pos = jnp.arange(length, dtype=jnp.int32)
    block_rows = math.gcd(tokens, 512)
    blocks = tokens // block_rows
    q_blocks = q_rot.reshape(blocks, block_rows, HQ, HD)
    pos_blocks = positions.reshape(blocks, block_rows)

    def score_block(query_blk, pos_blk):
        scores = jnp.einsum("thd,sd->hts", query_blk, all_keys, preferred_element_type=jnp.float32)
        causal = key_pos[None, None, :] <= pos_blk[None, :, None]
        return (scores, causal)

    def forward_block(operands):
        query_blk, pos_blk = operands
        scores, causal = score_block(query_blk, pos_blk)
        row_total = jnp.sum(jnp.where(causal, jnp.exp(scores), 0.0), axis=-1)
        log_total = jnp.log(row_total)
        attn_probs = jnp.where(causal, jnp.exp(scores - log_total[..., None]), 0.0).astype(
            jnp.bfloat16
        )
        attended = jnp.einsum(
            "hts,sd->thd", attn_probs, all_values, preferred_element_type=jnp.float32
        )
        return (attended, log_total)

    attended, log_totals = lax.map(forward_block, (q_blocks, pos_blocks))
    attn_b = attended.reshape(tokens, HQ * HD).astype(jnp.bfloat16)
    attn_proj = jnp.dot(attn_b, w_out, preferred_element_type=jnp.float32)
    attn_normed, attn_scale = rms_forward(attn_proj, norm_gains[1])
    hidden_one = input_rows + attn_normed
    ffn_in, ffn_scale = rms_forward(hidden_one, norm_gains[2])
    ffn_b = ffn_in.astype(jnp.bfloat16)
    gate_pre = jnp.dot(ffn_b, w_gate, preferred_element_type=jnp.float32)
    up_proj = jnp.dot(ffn_b, w_up, preferred_element_type=jnp.float32)
    activated = gelu_value(gate_pre)
    mixed_b = (activated * up_proj).astype(jnp.bfloat16)
    ffn_proj = jnp.dot(mixed_b, w_down, preferred_element_type=jnp.float32)
    ffn_normed, out_scale = rms_forward(ffn_proj, norm_gains[3])
    out_rows = (hidden_one + ffn_normed).astype(jnp.bfloat16)
    grad_rows = cotangent[0].astype(jnp.float32)
    d_ffn_proj, g_gain_three = rms_backward(ffn_proj, out_scale, norm_gains[3], grad_rows)
    d_ffn_b = d_ffn_proj.astype(jnp.bfloat16)
    grad_down = jnp.dot(mixed_b.T, d_ffn_b, preferred_element_type=jnp.float32)
    d_mixed = jnp.dot(d_ffn_b, w_down.T, preferred_element_type=jnp.float32)
    d_gate_b = (d_mixed * up_proj * gelu_slope(gate_pre)).astype(jnp.bfloat16)
    d_up_b = (d_mixed * activated).astype(jnp.bfloat16)
    grad_gate = jnp.dot(ffn_b.T, d_gate_b, preferred_element_type=jnp.float32)
    grad_up = jnp.dot(ffn_b.T, d_up_b, preferred_element_type=jnp.float32)
    d_ffn_in = jnp.dot(d_gate_b, w_gate.T, preferred_element_type=jnp.float32) + jnp.dot(
        d_up_b, w_up.T, preferred_element_type=jnp.float32
    )
    d_hidden_part, g_gain_two = rms_backward(hidden_one, ffn_scale, norm_gains[2], d_ffn_in)
    d_hidden_one = grad_rows + d_hidden_part
    d_attn_proj, g_gain_one = rms_backward(attn_proj, attn_scale, norm_gains[1], d_hidden_one)
    d_attn_b = d_attn_proj.astype(jnp.bfloat16)
    grad_out = jnp.dot(attn_b.T, d_attn_b, preferred_element_type=jnp.float32)
    d_heads = (
        jnp.dot(d_attn_b, w_out.T, preferred_element_type=jnp.float32)
        .astype(jnp.bfloat16)
        .reshape(tokens, HQ, HD)
    )
    attn_heads = attn_b.reshape(tokens, HQ, HD)
    row_delta = jnp.sum(d_heads.astype(jnp.float32) * attn_heads.astype(jnp.float32), axis=-1)
    delta_blocks = row_delta.reshape(blocks, block_rows, HQ)
    dout_blocks = d_heads.reshape(blocks, block_rows, HQ, HD)

    def backward_block(running, operands):
        key_acc, value_acc = running
        query_blk, pos_blk, lse_blk, dout_blk, delta_blk = operands
        scores, causal = score_block(query_blk, pos_blk)
        attn_probs = jnp.where(causal, jnp.exp(scores - lse_blk[..., None]), 0.0).astype(
            jnp.bfloat16
        )
        d_probs = jnp.einsum(
            "thd,sd->hts", dout_blk, all_values, preferred_element_type=jnp.float32
        )
        d_scores = (
            attn_probs.astype(jnp.float32) * (d_probs - jnp.transpose(delta_blk)[:, :, None])
        ).astype(jnp.bfloat16)
        value_acc = value_acc + jnp.einsum(
            "hts,thd->sd", attn_probs, dout_blk, preferred_element_type=jnp.float32
        )
        key_acc = key_acc + jnp.einsum(
            "hts,thd->sd", d_scores, query_blk, preferred_element_type=jnp.float32
        )
        d_query = jnp.einsum("hts,sd->thd", d_scores, all_keys, preferred_element_type=jnp.float32)
        return ((key_acc, value_acc), d_query)

    zero_rows = jnp.zeros((length, HD), jnp.float32)
    (key_terms, value_terms), d_queries = lax.scan(
        backward_block,
        (zero_rows, zero_rows),
        (q_blocks, pos_blocks, log_totals, dout_blocks, delta_blocks),
    )
    d_both = sum_rows(
        jnp.concatenate([key_terms, value_terms], axis=1).reshape(nc, tokens, 2 * HD), nc
    )
    d_keys, d_values = d_both[:, :HD], d_both[:, HD:]
    d_queries = d_queries.reshape(tokens, HQ, HD)
    d_q_normed = rotate_back(d_queries * query_scale, cos_tab[:, None, :], sin_tab[:, None, :])
    d_k_normed = rotate_back(d_keys, cos_tab, sin_tab)
    d_query_pre, g_head_query = rms_backward(queries, q_scale, head_gains[0], d_q_normed)
    d_key_pre, g_head_key = rms_backward(key_pre, k_scale, head_gains[1], d_k_normed)
    dq_b = d_query_pre.reshape(tokens, HQ * HD).astype(jnp.bfloat16)
    dk_b = d_key_pre.astype(jnp.bfloat16)
    dv_b = d_values.astype(jnp.bfloat16)
    grad_query = jnp.dot(normed_b.T, dq_b, preferred_element_type=jnp.float32)
    grad_key = jnp.dot(normed_b.T, dk_b, preferred_element_type=jnp.float32)
    grad_value = jnp.dot(normed_b.T, dv_b, preferred_element_type=jnp.float32)
    d_normed = (
        jnp.dot(dq_b, w_query.T, preferred_element_type=jnp.float32)
        + jnp.dot(dk_b, w_key.T, preferred_element_type=jnp.float32)
        + jnp.dot(dv_b, w_value.T, preferred_element_type=jnp.float32)
    )
    d_input_part, g_gain_zero = rms_backward(input_rows, in_scale, norm_gains[0], d_normed)
    d_input = (d_hidden_one + d_input_part)[None]
    packed, offsets = layout.pack(
        [
            grad_query,
            grad_key,
            grad_value,
            grad_out,
            grad_gate,
            grad_up,
            grad_down,
            jnp.stack([g_gain_zero, g_gain_one, g_gain_two, g_gain_three]),
            jnp.stack([g_head_query, g_head_key]),
        ]
    )
    total_params = layout.shards * layout.size
    summed, square_parts = reduce_grads(packed, offsets, layout, nd, nc, nz)
    summed = layout.pick(summed.reshape(layout.padded, LANES), owner)
    squares = jnp.sum(square_parts)
    new_params, new_first, new_second = adam_update(
        params, first_moment, second_moment, summed, clip_factor(squares, total_params)
    )
    return (out_rows[None], d_input, new_params, new_first, new_second, summed)


def solution(mesh):
    sizes = tuple(mesh.shape[axis] for axis in ("dp", "ctx", "zero"))
    placed = (
        P(("dp", "zero"), "ctx", None),
        P(("dp", "zero"), "ctx", None),
        P(("ctx", "zero")),
        P(("ctx", "zero")),
        P(("ctx", "zero")),
    )
    return jax.shard_map(
        functools.partial(local, sizes),
        mesh=mesh,
        in_specs=placed,
        out_specs=(
            P(("dp", "zero"), "ctx", None),
            P(("dp", "zero"), "ctx", None),
            P(("ctx", "zero")),
            P(("ctx", "zero")),
            P(("ctx", "zero")),
            P(("ctx", "zero")),
        ),
        check_vma=False,
    )
```

```python
import functools
import math

import jax
import jax.numpy as jnp
from jax import lax
from jax.experimental import pallas as pl
from jax.experimental.pallas import tpu as pltpu
from jax.sharding import PartitionSpec as P

D = 640
HQ = 4
HD = 256
FF = 2048


norm_eps = 1e-06
rope_base = 1000000.0
beta_one = 0.9
beta_two = 0.999
learn_rate = 0.01
decay_rate = 0.1
adam_eps = 1e-08
adam_step = 3
gelu_coef = 0.7978845608028654


def gelu_value(pre_act):
    tanh_part = jnp.tanh(gelu_coef * (pre_act + 0.044715 * pre_act * pre_act * pre_act))
    return 0.5 * pre_act * (1.0 + tanh_part)


def gelu_slope(pre_act):
    tanh_part = jnp.tanh(gelu_coef * (pre_act + 0.044715 * pre_act * pre_act * pre_act))
    return 0.5 * (1.0 + tanh_part) + 0.5 * pre_act * (1.0 - tanh_part * tanh_part) * gelu_coef * (
        1.0 + 3.0 * 0.044715 * pre_act * pre_act
    )


def rms_forward(values_in, gain_row):
    inv_rms = lax.rsqrt(jnp.mean(values_in * values_in, axis=-1, keepdims=True) + norm_eps)
    return (values_in * inv_rms * (1.0 + gain_row), inv_rms)


def rms_backward(values_in, inv_rms, gain_row, grad_out):
    weighted = grad_out * (1.0 + gain_row)
    grad_in = inv_rms * (
        weighted
        - values_in * inv_rms * inv_rms * jnp.mean(weighted * values_in, axis=-1, keepdims=True)
    )
    leading = tuple(range(values_in.ndim - 1))
    grad_gain = jnp.sum(grad_out * values_in * inv_rms, axis=leading)
    return (grad_in, grad_gain)


def rotary_tables(positions, head_dim):
    half_dim = head_dim // 2
    freqs = jnp.exp(
        jnp.arange(half_dim, dtype=jnp.float32) * (-2.0 * math.log(rope_base) / head_dim)
    )
    angles = positions.astype(jnp.float32)[:, None] * freqs[None, :]
    return (jnp.cos(angles), jnp.sin(angles))


def rotate(tensor, cos_part, sin_part):
    half_dim = tensor.shape[-1] // 2
    first_half = tensor[..., :half_dim]
    second_half = tensor[..., half_dim:]
    return jnp.concatenate(
        [
            first_half * cos_part - second_half * sin_part,
            second_half * cos_part + first_half * sin_part,
        ],
        axis=-1,
    )


def rotate_back(tensor, cos_part, sin_part):
    half_dim = tensor.shape[-1] // 2
    first_half = tensor[..., :half_dim]
    second_half = tensor[..., half_dim:]
    return jnp.concatenate(
        [
            first_half * cos_part + second_half * sin_part,
            second_half * cos_part - first_half * sin_part,
        ],
        axis=-1,
    )


def weight_layouts(model_width, head_count, head_dim, hidden):
    return [
        (model_width, head_count * head_dim),
        (model_width, head_dim),
        (model_width, head_dim),
        (head_count * head_dim, model_width),
        (model_width, hidden),
        (model_width, hidden),
        (hidden, model_width),
        (4, model_width),
        (2, head_dim),
    ]


def unpack(flat_values, model_width, head_count, head_dim, hidden):
    layouts = weight_layouts(model_width, head_count, head_dim, hidden)
    pieces = []
    offset = 0
    for layout in layouts:
        amount = layout[0] * layout[1]
        pieces.append(flat_values[offset : offset + amount].reshape(layout))
        offset += amount
    return pieces


def adam_update(weights, moment_one, moment_two, grad_values, clip_scale):
    clipped = grad_values * clip_scale
    new_one = beta_one * moment_one + (1.0 - beta_one) * clipped
    new_two = beta_two * moment_two + (1.0 - beta_two) * clipped * clipped
    corrected_one = new_one / (1.0 - beta_one**adam_step)
    corrected_two = new_two / (1.0 - beta_two**adam_step)
    new_weights = weights - learn_rate * (
        corrected_one / (jnp.sqrt(corrected_two) + adam_eps) + decay_rate * weights
    )
    return (new_weights, new_one, new_two)


def clip_factor(squares, amount):
    return jnp.minimum(1.0, lax.rsqrt(squares / amount + 1e-06))


MESH_ID = pl.DeviceIdType.MESH
LANES = 128
VMEM_LIMIT = 60 * 1024 * 1024


def ring(position, step, size):
    return lax.rem(position + step, size)


def back(position, step, size):
    return lax.rem(position + size - step, size)


def greet(peers):
    barrier = pltpu.get_barrier_semaphore()
    for peer in peers:
        pl.semaphore_signal(barrier, inc=1, device_id=peer, device_id_type=MESH_ID)
    pl.semaphore_wait(barrier, len(peers))


def remote(src, dst, send_sem, recv_sem, peer):
    return pltpu.make_async_remote_copy(
        src_ref=src,
        dst_ref=dst,
        send_sem=send_sem,
        recv_sem=recv_sem,
        device_id=peer,
        device_id_type=MESH_ID,
    )


def quarter(ref, part, rows, first=0, amount=None):
    amount = rows if amount is None else amount
    return ref.at[pl.ds(pl.multiple_of(part * rows + first, ALIGN), amount)]


def square(d):
    return d + 1 - 2 * lax.rem(d, 2), lax.rem(d + 2, 4)


def gather_kernel(nd, nc, nz, layout, plan, x_ref, *refs):
    outs = refs[: len(plan)]
    full_ref, own_sem, s1s, s1r, s2s, s2r, s3s, s3r, sos, sor, out_sem = refs[len(plan) :]
    d = lax.axis_index("dp")
    c = lax.axis_index("ctx")
    z = lax.axis_index("zero")
    rows = layout.part
    half = rows // 2
    greet(
        [{"zero": ring(z, k, nz)} for k in range(1, nz)]
        + [{"dp": ring(d, i, nd)} for i in range(1, nd)]
        + [{"ctx": ring(c, j, nc)} for j in range(1, nc)]
    )
    sends = []

    def start(src, dst, ssem, rsem, peer):
        copy = remote(src, dst, ssem, rsem, peer)
        copy.start()
        sends.append(copy)

    def piece_of(col, row, part, first=0, amount=None):
        return quarter(full_ref.at[col, row], part, rows, first, amount)

    def arrived(ref, sem, peer):
        remote(ref, ref, s1s.at[0], sem, peer).wait_recv()

    for k in range(1, nz):
        start(
            quarter(x_ref, d, rows), piece_of(c, z, d), s1s.at[k], s1r.at[k],
            {"zero": ring(z, k, nz)},
        )
    own = pltpu.make_async_copy(x_ref, full_ref.at[c, z], own_sem)
    own.start()
    for j in range(1, nc):
        start(x_ref, full_ref.at[c, z], sos.at[j], sor.at[j], {"ctx": ring(c, j, nc)})

    def to_ctx(piece, k, i):
        for j in range(1, nc):
            start(piece, piece, s3s.at[k, i, j], s3r.at[k, i, j], {"ctx": ring(c, j, nc)})

    paired = nd == 4
    if paired:
        near_x, near_y = square(d)
        far = 3 - d
        hops = [(1, near_x), (2, near_y)]
    else:
        hops = [(i, ring(d, i, nd)) for i in range(1, nd)]
    for k in range(1, nz):
        piece = piece_of(c, back(z, k, nz), d)
        arrived(piece, s1r.at[k], {"zero": ring(z, k, nz)})
        for i, peer in hops:
            start(piece, piece, s2s.at[k, i], s2r.at[k, i], {"dp": peer})
        to_ctx(piece, k, 0)
    for k in range(1, nz):
        src_z = back(z, k, nz)
        for i, peer in hops:
            origin = peer if paired else back(d, i, nd)
            piece = piece_of(c, src_z, origin)
            arrived(piece, s2r.at[k, i], {"dp": peer})
            if paired:
                onward = piece_of(c, src_z, origin, (i - 1) * half, half)
                other = near_y if i == 1 else near_x
                start(onward, onward, s2s.at[k, 2 + i], s2r.at[k, 2 + i], {"dp": other})
            to_ctx(piece, k, i)
    if paired:
        for k in range(1, nz):
            src_z = back(z, k, nz)
            for i, peer in ((1, near_y), (2, near_x)):
                piece = piece_of(c, src_z, far, (i - 1) * half, half)
                arrived(piece, s2r.at[k, 2 + i], {"dp": peer})
            to_ctx(piece_of(c, src_z, far), k, 3)
    for j in range(1, nc):
        src_c = back(c, j, nc)
        peer = {"ctx": ring(c, j, nc)}
        arrived(full_ref.at[src_c, z], sor.at[j], peer)
        for k in range(1, nz):
            src_z = back(z, k, nz)
            if paired:
                origins = (d, near_x, near_y, far)
            else:
                origins = [back(d, i, nd) for i in range(nd)]
            for i, origin in enumerate(origins):
                arrived(piece_of(src_c, src_z, origin), s3r.at[k, i, j], peer)
    for copy in sends:
        copy.wait_send()
    own.wait()
    for index in range(layout.shards - 1):
        if layout.lead(index + 1):
            tail = pl.ds(layout.base(index + 1) - layout.base(index), ALIGN)
            here = divmod(index, nz)
            there = divmod(index + 1, nz)
            full_ref[here[0], here[1], tail, :] = (
                full_ref[here[0], here[1], tail, :] + full_ref[there[0], there[1], pl.ds(0, ALIGN), :]
            )
    moves = []
    for out, segments in zip(outs, plan):
        for index, src, dst, amount in segments:
            move = pltpu.make_async_copy(
                full_ref.at[index // nz, index % nz, pl.ds(src, amount)],
                out.at[pl.ds(dst, amount)],
                out_sem.at[len(moves)],
            )
            move.start()
            moves.append(move)
    for move in moves:
        move.wait()


def gather_weights(x, layout, plan, nd, nc, nz):
    dma = pltpu.SemaphoreType.DMA
    anywhere = pl.BlockSpec(memory_space=pl.ANY)
    return pl.pallas_call(
        functools.partial(gather_kernel, nd, nc, nz, layout, plan),
        out_shape=[
            jax.ShapeDtypeStruct((sum(part[3] for part in segments), LANES), x.dtype)
            for segments in plan
        ],
        in_specs=[pl.BlockSpec(memory_space=pltpu.VMEM)],
        out_specs=[anywhere] * len(plan),
        scratch_shapes=[
            pltpu.VMEM((nc, nz, layout.padded, LANES), x.dtype),
            dma,
            dma((nz,)),
            dma((nz,)),
            dma((nz, nd + 1)),
            dma((nz, nd + 1)),
            dma((nz, nd, nc)),
            dma((nz, nd, nc)),
            dma((nc,)),
            dma((nc,)),
            dma((sum(len(segments) for segments in plan),)),
        ],
        compiler_params=pltpu.CompilerParams(
            collective_id=0, has_side_effects=True, vmem_limit_bytes=VMEM_LIMIT
        ),
        name="gather_weights",
    )(x)


def reduce_kernel(
    nd, nc, nz, layout, offsets, *refs
):
    g_parts = refs[: len(offsets)]
    (
        out_ref, sq_ref, g_ref, a_buf, b_src, b_buf, b_mid, b_two, c_src, c_buf, d_buf,
        g_sem, sas, sar, sbs, sbr, scs, scr, sds, sdr, sqs, sqr,
    ) = refs[len(offsets) :]
    loads = []
    for index, offset in enumerate(offsets):
        load = pltpu.make_async_copy(
            g_parts[index],
            g_ref.at[pl.ds(offset, g_parts[index].shape[0])],
            g_sem.at[index],
        )
        load.start()
        loads.append(load)
    d = lax.axis_index("dp")
    c = lax.axis_index("ctx")
    z = lax.axis_index("zero")
    step_rows = 32
    rows = layout.part
    wide = nd * step_rows

    def base(col, row):
        return pl.multiple_of(layout.base(col * nz + row), ALIGN)

    greet(
        [
            {"ctx": ring(c, j, nc), "zero": ring(z, k, nz)}
            for j in range(nc)
            for k in range(nz)
            if j or k
        ]
        + [{"dp": ring(d, i, nd)} for i in range(1, nd)]
    )
    sends = []

    def start(src, dst, ssem, rsem, peer):
        copy = remote(src, dst, ssem, rsem, peer)
        copy.start()
        sends.append(copy)
        return copy

    for load in loads:
        load.wait()
    paired = nd == 4
    half = rows // 2
    if paired:
        near_x, near_y = square(d)
        far = 3 - d
    first = []
    for k in range(nz):
        dst_z = ring(z, k + 1, nz)
        first.append(
            [
                start(
                    g_ref.at[pl.ds(base(ring(c, j, nc), dst_z), layout.padded)],
                    a_buf.at[k, j - 1],
                    sas.at[k, j],
                    sar.at[k, j],
                    {"ctx": ring(c, j, nc)},
                )
                for j in range(1, nc)
            ]
        )
    second = []
    for k in range(nz):
        dst_z = ring(z, k + 1, nz)
        for copy in first[k]:
            copy.wait_recv()

        def add_ctx(r, carry, k=k, dst_z=dst_z):
            at = pl.ds(pl.multiple_of(r * wide, ALIGN), wide)
            mine = pl.ds(pl.multiple_of(base(c, dst_z) + r * wide, ALIGN), wide)
            total = g_ref[mine, :].astype(jnp.float32)
            for j in range(1, nc):
                total = total + a_buf[k, j - 1, at, :].astype(jnp.float32)
            b_src[k, at, :] = total.astype(jnp.bfloat16)
            return carry

        lax.fori_loop(0, layout.padded // wide, add_ctx, 0)
        if paired:
            second.append(
                [
                    start(
                        quarter(b_src.at[k], part, rows, lot * half, half),
                        b_buf.at[k, 2 * lot + place],
                        sbs.at[k, 2 * lot + place],
                        sbr.at[k, 2 * lot + place],
                        {"dp": peer},
                    )
                    for lot, place, part, peer in (
                        (0, 1, far, near_x),
                        (1, 1, far, near_y),
                        (0, 0, near_x, near_x),
                        (1, 0, near_y, near_y),
                    )
                ]
            )
            continue
        second.append(
            [
                start(
                    b_src.at[k, pl.ds(pl.multiple_of(ring(d, i, nd) * rows, 32), rows)],
                    b_buf.at[k, i - 1],
                    sbs.at[k, i],
                    sbr.at[k, i],
                    {"dp": ring(d, i, nd)},
                )
                for i in range(1, nd)
            ]
        )
    middle = []
    for k in range(nz if paired else 0):
        for copy in second[k]:
            copy.wait_recv()

        def add_near(r, carry, k=k):
            at = pl.ds(0, half)
            for lot, part in ((0, near_y), (1, near_x)):
                mine = pl.ds(
                    pl.multiple_of(part * rows + lot * half, ALIGN), half
                )
                total = b_src[k, mine, :].astype(jnp.float32)
                total = total + b_buf[k, 2 * lot + 1, at, :].astype(jnp.float32)
                b_mid[k, lot, at, :] = total.astype(jnp.bfloat16)
            return carry

        add_near(0, 0)
        middle.append(
            [
                start(
                    b_mid.at[k, lot],
                    b_two.at[k, lot],
                    sbs.at[k, 4 + lot],
                    sbr.at[k, 4 + lot],
                    {"dp": peer},
                )
                for lot, peer in ((0, near_y), (1, near_x))
            ]
        )
    third = []
    for k in range(nz):
        for copy in middle[k] if paired else second[k]:
            copy.wait_recv()

        def add_dp(r, carry, k=k):
            at = pl.ds(pl.multiple_of(r * step_rows, step_rows), step_rows)
            mine = pl.ds(pl.multiple_of(d * rows + r * step_rows, step_rows), step_rows)
            total = b_src[k, mine, :].astype(jnp.float32)
            for i in range(1, nd):
                total = total + b_buf[k, i - 1, at, :].astype(jnp.float32)
            c_src[k, at, :] = total.astype(jnp.bfloat16)
            return carry

        def add_pair(r, carry, k=k):
            at = pl.ds(0, half)
            for lot in range(2):
                mine = pl.ds(pl.multiple_of(d * rows + lot * half, ALIGN), half)
                total = b_src[k, mine, :].astype(jnp.float32)
                total = total + b_buf[k, 2 * lot, at, :].astype(jnp.float32)
                total = total + b_two[k, lot, at, :].astype(jnp.float32)
                put = pl.ds(lot * half, half)
                c_src[k, put, :] = total.astype(jnp.bfloat16)
            return carry

        if paired:
            add_pair(0, 0)
        else:
            lax.fori_loop(0, rows // step_rows, add_dp, 0)
        if k < nz - 1:
            third.append(
                start(
                    c_src.at[k],
                    c_buf.at[k],
                    scs.at[k],
                    scr.at[k],
                    {"zero": ring(z, k + 1, nz)},
                )
            )
    for copy in third:
        copy.wait_recv()

    def add_zero(r, carry):
        at = pl.ds(pl.multiple_of(r * step_rows, step_rows), step_rows)
        total = c_src[nz - 1, at, :].astype(jnp.float32)
        for k in range(nz - 1):
            total = total + c_buf[k, at, :].astype(jnp.float32)
        d_buf[d, at, :] = total.astype(jnp.bfloat16)
        return carry

    lax.fori_loop(0, rows // step_rows, add_zero, 0)
    mine = d_buf.at[d]
    for i in range(1, nd):
        start(mine, mine, sds.at[i], sdr.at[i], {"dp": ring(d, i, nd)})
    for i in range(1, nd):
        theirs = d_buf.at[back(d, i, nd)]
        remote(theirs, theirs, sds.at[i], sdr.at[i], {"dp": ring(d, i, nd)}).wait_recv()

    lead = layout.lead(c * nz + z)

    def finish(r, carry):
        at = pl.ds(pl.multiple_of(r * step_rows, step_rows), step_rows)
        total = d_buf[:, at, :].astype(jnp.float32)
        index = (
            lax.broadcasted_iota(jnp.int32, total.shape, 0) * rows
            + lax.broadcasted_iota(jnp.int32, total.shape, 1)
            + r * step_rows
        )
        total = jnp.where((index >= lead) & (index < lead + layout.used), total, 0.0)
        out_ref[:, at, :] = total
        return carry + jnp.sum((total * total).reshape(-1, 8, LANES), axis=0)

    sq_ref[0] = lax.fori_loop(
        0, rows // step_rows, finish, jnp.zeros((8, LANES), jnp.float32)
    )
    last = []
    for j in range(nc):
        for k in range(nz):
            slot = j * nz + k
            if slot:
                last.append(
                    start(
                        sq_ref.at[0],
                        sq_ref.at[slot],
                        sqs.at[slot],
                        sqr.at[slot],
                        {"ctx": ring(c, j, nc), "zero": ring(z, k, nz)},
                    )
                )
    for copy in last:
        copy.wait_recv()
    for copy in sends:
        copy.wait_send()


def reduce_grads(parts, offsets, layout, nd, nc, nz):
    dma = pltpu.SemaphoreType.DMA
    rows = layout.part
    vmem = pl.BlockSpec(memory_space=pltpu.VMEM)
    return pl.pallas_call(
        functools.partial(reduce_kernel, nd, nc, nz, layout, offsets),
        out_shape=(
            jax.ShapeDtypeStruct((nd, rows, LANES), jnp.float32),
            jax.ShapeDtypeStruct((nc * nz, 8, LANES), jnp.float32),
        ),
        in_specs=[pl.BlockSpec(memory_space=pl.ANY)] * len(parts),
        out_specs=(vmem, vmem),
        scratch_shapes=[
            pltpu.VMEM((layout.total, LANES), jnp.bfloat16),
            pltpu.VMEM((nz, max(nc - 1, 1), layout.padded, LANES), jnp.bfloat16),
            pltpu.VMEM((nz, layout.padded, LANES), jnp.bfloat16),
            pltpu.VMEM(
                (nz, 4, rows // 2, LANES) if nd == 4 else (nz, max(nd - 1, 1), rows, LANES),
                jnp.bfloat16,
            ),
            pltpu.VMEM((nz, 2, rows // 2, LANES), jnp.bfloat16),
            pltpu.VMEM((nz, 2, rows // 2, LANES), jnp.bfloat16),
            pltpu.VMEM((nz, rows, LANES), jnp.bfloat16),
            pltpu.VMEM((nz, rows, LANES), jnp.bfloat16),
            pltpu.VMEM((nd, rows, LANES), jnp.bfloat16),
            dma((len(parts),)),
            dma((nz, nc)),
            dma((nz, nc)),
            dma((nz, nd + 2)),
            dma((nz, nd + 2)),
            dma((nz,)),
            dma((nz,)),
            dma((nd,)),
            dma((nd,)),
            dma((nc * nz,)),
            dma((nc * nz,)),
        ],
        compiler_params=pltpu.CompilerParams(
            collective_id=1, has_side_effects=True, vmem_limit_bytes=VMEM_LIMIT
        ),
        name="reduce_grads",
    )(*parts)


def share_kernel(nc, x_ref, out_ref, buf, own_sem, ssem, rsem):
    c = lax.axis_index("ctx")
    greet([{"ctx": ring(c, j, nc)} for j in range(1, nc)])
    copies = []
    for j in range(1, nc):
        copy = remote(x_ref, buf.at[j - 1], ssem.at[j], rsem.at[j], {"ctx": ring(c, j, nc)})
        copy.start()
        copies.append(copy)
    out_ref[c] = x_ref[...]
    for j in range(1, nc):
        copies[j - 1].wait()
        out_ref[back(c, j, nc)] = buf[j - 1]


def share_rows(x, nc):
    dma = pltpu.SemaphoreType.DMA
    vmem = pl.BlockSpec(memory_space=pltpu.VMEM)
    return pl.pallas_call(
        functools.partial(share_kernel, nc),
        out_shape=jax.ShapeDtypeStruct((nc,) + x.shape, x.dtype),
        in_specs=[vmem],
        out_specs=vmem,
        scratch_shapes=[
            pltpu.VMEM((max(nc - 1, 1),) + x.shape, x.dtype),
            dma,
            dma((nc,)),
            dma((nc,)),
        ],
        compiler_params=pltpu.CompilerParams(collective_id=2, has_side_effects=True),
        name="share_rows",
    )(x)


def sum_kernel(nc, x_ref, out_ref, buf, ssem, rsem):
    c = lax.axis_index("ctx")
    greet([{"ctx": ring(c, j, nc)} for j in range(1, nc)])
    copies = []
    for j in range(1, nc):
        copy = remote(
            x_ref.at[ring(c, j, nc)],
            buf.at[j - 1],
            ssem.at[j],
            rsem.at[j],
            {"ctx": ring(c, j, nc)},
        )
        copy.start()
        copies.append(copy)
    total = x_ref[c]
    for j in range(1, nc):
        copies[j - 1].wait()
        total = total + buf[j - 1]
    out_ref[...] = total


def sum_rows(x, nc):
    dma = pltpu.SemaphoreType.DMA
    vmem = pl.BlockSpec(memory_space=pltpu.VMEM)
    return pl.pallas_call(
        functools.partial(sum_kernel, nc),
        out_shape=jax.ShapeDtypeStruct(x.shape[1:], x.dtype),
        in_specs=[vmem],
        out_specs=vmem,
        scratch_shapes=[
            pltpu.VMEM((max(nc - 1, 1),) + x.shape[1:], x.dtype),
            dma((nc,)),
            dma((nc,)),
        ],
        compiler_params=pltpu.CompilerParams(collective_id=3, has_side_effects=True),
        name="sum_rows",
    )(x)


ALIGN = 16


class ShardRows:
    def __init__(self, shard_size, shards, parts):
        self.size = shard_size
        self.shards = shards
        self.whole = shard_size % LANES == 0
        self.used = -(-shard_size // LANES)
        spare = ALIGN - 1 if self.whole else 0
        self.part = -(-(self.used + spare) // (parts * 32)) * 32
        self.padded = parts * self.part
        self.total = self.base(shards - 1) + self.padded

    def base(self, index):
        if self.whole:
            return index * self.used // ALIGN * ALIGN
        return index * self.padded

    def lead(self, index):
        return index * self.used % ALIGN if self.whole else index * 0

    def place(self, flat, index):
        if not self.whole:
            extra = self.padded * LANES - self.size
            return jnp.pad(flat, (0, extra)).reshape(self.padded, LANES).astype(jnp.bfloat16)
        held = jnp.zeros((self.padded, LANES), flat.dtype)
        held = lax.dynamic_update_slice(
            held, flat.reshape(self.used, LANES), (self.lead(index), 0)
        )
        return held.astype(jnp.bfloat16)

    def pick(self, held, index):
        if not self.whole:
            return held.reshape(-1)[: self.size]
        return lax.dynamic_slice(held, (self.lead(index), 0), (self.used, LANES)).reshape(-1)

    def begin(self, index):
        return self.base(index) + (ALIGN if self.lead(index) else 0)

    def segments(self, low, high):
        found = []
        for index in range(self.shards):
            last = self.base(index) + self.padded
            if index + 1 < self.shards:
                last = self.begin(index + 1)
            first, last = max(self.begin(index), low), min(last, high)
            if first < last:
                found.append((index, first - self.base(index), first - low, last - first))
        return found

    def plan(self, layouts):
        if not self.whole:
            return [self.segments(0, self.total)]
        low = 0
        plans = []
        for layout in layouts[:-2]:
            amount = layout[0] * layout[1] // LANES
            plans.append(self.segments(low, low + amount))
            low += amount
        high = -(-self.shards * self.used // ALIGN) * ALIGN
        plans.append(self.segments(low, high))
        return plans

    def unpack(self, taken, layouts, sizes):
        if not self.whole:
            flat = taken[0].reshape(self.shards, -1)[:, : self.size].reshape(-1)
            return unpack(flat, *sizes)
        pieces = [rows.reshape(layout) for rows, layout in zip(taken, layouts[:-2])]
        gains = taken[-1].reshape(-1)
        low = 0
        for layout in layouts[-2:]:
            amount = layout[0] * layout[1]
            pieces.append(gains[low : low + amount].reshape(layout))
            low += amount
        return pieces

    def pack(self, grads):
        if not self.whole:
            flat = jnp.concatenate([grad.reshape(-1) for grad in grads]).astype(jnp.bfloat16)
            flat = jnp.pad(
                flat.reshape(self.shards, -1), ((0, 0), (0, self.padded * LANES - self.size))
            )
            return [flat.reshape(self.total, LANES)], [0]
        parts = [grad.astype(jnp.bfloat16).reshape(-1, LANES) for grad in grads[:-2]]
        offsets = [0]
        for part in parts:
            offsets.append(offsets[-1] + part.shape[0])
        small = jnp.concatenate([grad.reshape(-1) for grad in grads[-2:]])
        small = small.astype(jnp.bfloat16).reshape(-1, LANES)
        spare = self.total - offsets[-1] - small.shape[0]
        parts.append(jnp.pad(small, ((0, spare), (0, 0))))
        return parts, offsets


def local(sizes, inputs, cotangent, params, first_moment, second_moment):
    tokens = inputs.shape[1]
    nd, nc, nz = sizes
    owner = lax.axis_index("ctx") * nz + lax.axis_index("zero")
    layout = ShardRows(params.shape[0], nc * nz, nd)
    layouts = weight_layouts(D, HQ, HD, FF)
    own_b = layout.place(params, owner)
    gathered = gather_weights(own_b, layout, layout.plan(layouts), nd, nc, nz)
    w_query, w_key, w_value, w_out, w_gate, w_up, w_down, norm_gains, head_gains = layout.unpack(
        gathered, layouts, (D, HQ, HD, FF)
    )
    norm_gains = norm_gains.astype(jnp.float32)
    head_gains = head_gains.astype(jnp.float32)
    positions = lax.axis_index("ctx") * tokens + jnp.arange(tokens, dtype=jnp.int32)
    cos_tab, sin_tab = rotary_tables(positions, HD)
    input_rows = inputs[0].astype(jnp.float32)
    normed_in, in_scale = rms_forward(input_rows, norm_gains[0])
    normed_b = normed_in.astype(jnp.bfloat16)
    queries = jnp.dot(normed_b, w_query, preferred_element_type=jnp.float32).reshape(tokens, HQ, HD)
    key_pre = jnp.dot(normed_b, w_key, preferred_element_type=jnp.float32)
    values = jnp.dot(normed_b, w_value, preferred_element_type=jnp.float32)
    q_normed, q_scale = rms_forward(queries, head_gains[0])
    k_normed, k_scale = rms_forward(key_pre, head_gains[1])
    query_scale = HD ** (-0.5)
    q_rot = (rotate(q_normed, cos_tab[:, None, :], sin_tab[:, None, :]) * query_scale).astype(
        jnp.bfloat16
    )
    k_rot = rotate(k_normed, cos_tab, sin_tab).astype(jnp.bfloat16)
    v_rows = values.astype(jnp.bfloat16)
    shared = share_rows(jnp.concatenate([k_rot, v_rows], axis=1), nc).reshape(nc * tokens, 2 * HD)
    all_keys, all_values = shared[:, :HD], shared[:, HD:]
    length = all_keys.shape[0]
    key_pos = jnp.arange(length, dtype=jnp.int32)
    block_rows = math.gcd(tokens, 512)
    blocks = tokens // block_rows
    q_blocks = q_rot.reshape(blocks, block_rows, HQ, HD)
    pos_blocks = positions.reshape(blocks, block_rows)

    def score_block(query_blk, pos_blk):
        scores = jnp.einsum("thd,sd->hts", query_blk, all_keys, preferred_element_type=jnp.float32)
        causal = key_pos[None, None, :] <= pos_blk[None, :, None]
        return (scores, causal)

    def forward_block(operands):
        query_blk, pos_blk = operands
        scores, causal = score_block(query_blk, pos_blk)
        row_total = jnp.sum(jnp.where(causal, jnp.exp(scores), 0.0), axis=-1)
        log_total = jnp.log(row_total)
        attn_probs = jnp.where(causal, jnp.exp(scores - log_total[..., None]), 0.0).astype(
            jnp.bfloat16
        )
        attended = jnp.einsum(
            "hts,sd->thd", attn_probs, all_values, preferred_element_type=jnp.float32
        )
        return (attended, log_total)

    attended, log_totals = lax.map(forward_block, (q_blocks, pos_blocks))
    attn_b = attended.reshape(tokens, HQ * HD).astype(jnp.bfloat16)
    attn_proj = jnp.dot(attn_b, w_out, preferred_element_type=jnp.float32)
    attn_normed, attn_scale = rms_forward(attn_proj, norm_gains[1])
    hidden_one = input_rows + attn_normed
    ffn_in, ffn_scale = rms_forward(hidden_one, norm_gains[2])
    ffn_b = ffn_in.astype(jnp.bfloat16)
    gate_pre = jnp.dot(ffn_b, w_gate, preferred_element_type=jnp.float32)
    up_proj = jnp.dot(ffn_b, w_up, preferred_element_type=jnp.float32)
    activated = gelu_value(gate_pre)
    mixed_b = (activated * up_proj).astype(jnp.bfloat16)
    ffn_proj = jnp.dot(mixed_b, w_down, preferred_element_type=jnp.float32)
    ffn_normed, out_scale = rms_forward(ffn_proj, norm_gains[3])
    out_rows = (hidden_one + ffn_normed).astype(jnp.bfloat16)
    grad_rows = cotangent[0].astype(jnp.float32)
    d_ffn_proj, g_gain_three = rms_backward(ffn_proj, out_scale, norm_gains[3], grad_rows)
    d_ffn_b = d_ffn_proj.astype(jnp.bfloat16)
    grad_down = jnp.dot(mixed_b.T, d_ffn_b, preferred_element_type=jnp.float32)
    d_mixed = jnp.dot(d_ffn_b, w_down.T, preferred_element_type=jnp.float32)
    d_gate_b = (d_mixed * up_proj * gelu_slope(gate_pre)).astype(jnp.bfloat16)
    d_up_b = (d_mixed * activated).astype(jnp.bfloat16)
    grad_gate = jnp.dot(ffn_b.T, d_gate_b, preferred_element_type=jnp.float32)
    grad_up = jnp.dot(ffn_b.T, d_up_b, preferred_element_type=jnp.float32)
    d_ffn_in = jnp.dot(d_gate_b, w_gate.T, preferred_element_type=jnp.float32) + jnp.dot(
        d_up_b, w_up.T, preferred_element_type=jnp.float32
    )
    d_hidden_part, g_gain_two = rms_backward(hidden_one, ffn_scale, norm_gains[2], d_ffn_in)
    d_hidden_one = grad_rows + d_hidden_part
    d_attn_proj, g_gain_one = rms_backward(attn_proj, attn_scale, norm_gains[1], d_hidden_one)
    d_attn_b = d_attn_proj.astype(jnp.bfloat16)
    grad_out = jnp.dot(attn_b.T, d_attn_b, preferred_element_type=jnp.float32)
    d_heads = (
        jnp.dot(d_attn_b, w_out.T, preferred_element_type=jnp.float32)
        .astype(jnp.bfloat16)
        .reshape(tokens, HQ, HD)
    )
    attn_heads = attn_b.reshape(tokens, HQ, HD)
    row_delta = jnp.sum(d_heads.astype(jnp.float32) * attn_heads.astype(jnp.float32), axis=-1)
    delta_blocks = row_delta.reshape(blocks, block_rows, HQ)
    dout_blocks = d_heads.reshape(blocks, block_rows, HQ, HD)

    def backward_block(running, operands):
        key_acc, value_acc = running
        query_blk, pos_blk, lse_blk, dout_blk, delta_blk = operands
        scores, causal = score_block(query_blk, pos_blk)
        attn_probs = jnp.where(causal, jnp.exp(scores - lse_blk[..., None]), 0.0).astype(
            jnp.bfloat16
        )
        d_probs = jnp.einsum(
            "thd,sd->hts", dout_blk, all_values, preferred_element_type=jnp.float32
        )
        d_scores = (
            attn_probs.astype(jnp.float32) * (d_probs - jnp.transpose(delta_blk)[:, :, None])
        ).astype(jnp.bfloat16)
        value_acc = value_acc + jnp.einsum(
            "hts,thd->sd", attn_probs, dout_blk, preferred_element_type=jnp.float32
        )
        key_acc = key_acc + jnp.einsum(
            "hts,thd->sd", d_scores, query_blk, preferred_element_type=jnp.float32
        )
        d_query = jnp.einsum("hts,sd->thd", d_scores, all_keys, preferred_element_type=jnp.float32)
        return ((key_acc, value_acc), d_query)

    zero_rows = jnp.zeros((length, HD), jnp.float32)
    (key_terms, value_terms), d_queries = lax.scan(
        backward_block,
        (zero_rows, zero_rows),
        (q_blocks, pos_blocks, log_totals, dout_blocks, delta_blocks),
    )
    d_both = sum_rows(
        jnp.concatenate([key_terms, value_terms], axis=1).reshape(nc, tokens, 2 * HD), nc
    )
    d_keys, d_values = d_both[:, :HD], d_both[:, HD:]
    d_queries = d_queries.reshape(tokens, HQ, HD)
    d_q_normed = rotate_back(d_queries * query_scale, cos_tab[:, None, :], sin_tab[:, None, :])
    d_k_normed = rotate_back(d_keys, cos_tab, sin_tab)
    d_query_pre, g_head_query = rms_backward(queries, q_scale, head_gains[0], d_q_normed)
    d_key_pre, g_head_key = rms_backward(key_pre, k_scale, head_gains[1], d_k_normed)
    dq_b = d_query_pre.reshape(tokens, HQ * HD).astype(jnp.bfloat16)
    dk_b = d_key_pre.astype(jnp.bfloat16)
    dv_b = d_values.astype(jnp.bfloat16)
    grad_query = jnp.dot(normed_b.T, dq_b, preferred_element_type=jnp.float32)
    grad_key = jnp.dot(normed_b.T, dk_b, preferred_element_type=jnp.float32)
    grad_value = jnp.dot(normed_b.T, dv_b, preferred_element_type=jnp.float32)
    d_normed = (
        jnp.dot(dq_b, w_query.T, preferred_element_type=jnp.float32)
        + jnp.dot(dk_b, w_key.T, preferred_element_type=jnp.float32)
        + jnp.dot(dv_b, w_value.T, preferred_element_type=jnp.float32)
    )
    d_input_part, g_gain_zero = rms_backward(input_rows, in_scale, norm_gains[0], d_normed)
    d_input = (d_hidden_one + d_input_part)[None]
    packed, offsets = layout.pack(
        [
            grad_query,
            grad_key,
            grad_value,
            grad_out,
            grad_gate,
            grad_up,
            grad_down,
            jnp.stack([g_gain_zero, g_gain_one, g_gain_two, g_gain_three]),
            jnp.stack([g_head_query, g_head_key]),
        ]
    )
    total_params = layout.shards * layout.size
    summed, square_parts = reduce_grads(packed, offsets, layout, nd, nc, nz)
    summed = layout.pick(summed.reshape(layout.padded, LANES), owner)
    squares = jnp.sum(square_parts)
    new_params, new_first, new_second = adam_update(
        params, first_moment, second_moment, summed, clip_factor(squares, total_params)
    )
    return (out_rows[None], d_input, new_params, new_first, new_second, summed)


def solution(mesh):
    sizes = tuple(mesh.shape[axis] for axis in ("dp", "ctx", "zero"))
    placed = (
        P(("dp", "zero"), "ctx", None),
        P(("dp", "zero"), "ctx", None),
        P(("ctx", "zero")),
        P(("ctx", "zero")),
        P(("ctx", "zero")),
    )
    return jax.shard_map(
        functools.partial(local, sizes),
        mesh=mesh,
        in_specs=placed,
        out_specs=(
            P(("dp", "zero"), "ctx", None),
            P(("dp", "zero"), "ctx", None),
            P(("ctx", "zero")),
            P(("ctx", "zero")),
            P(("ctx", "zero")),
            P(("ctx", "zero")),
        ),
        check_vma=False,
    )
```
